768 devices in a mesh: ctx: 48 (over y_hi, z), head: 16 (over x, y_lo, core).
Axes of the slice: x: 4, y: 8 (y_hi: 4, y_lo: 2; y = y_hi * 2 + y_lo), z: 12, core: 2. Of those that a mesh axis runs over, the one named last changes fastest.
Arguments:
- queries: bfloat16 [6144, 8192], P('ctx', 'head'), may hold values from -224 to 224
- key_rows: bfloat16 [6144, 1024], P('ctx'), may hold values from -16 to 16
- value_rows: bfloat16 [6144, 1024], P('ctx'), may hold values from -6 to 6
- block_flags: int32 [96, 96], P('ctx'), may hold values from 0 to 1, as said below
- out_weight: bfloat16 [8192, 8192], P('head'), may hold values from -0.125 to 0.125
Outputs:
- projected: bfloat16 [6144, 8192], P(('ctx', 'head'))
The draws below stay inside these ranges and needn't reach their ends.
Inputs may be any that keep to these rules, and one draw needn't show every extreme that they name: `block_flags`: 0 or 1; zero above the diagonal, one on it.
All inputs are finite; a program needn't handle non-finite values.
Results may differ from the reference program's by a relative error of at most 0.0085.
Values may be sent and summed in bfloat16 or wider, within the bound.
A program may use at most 32 MiB of HBM per device.

```python
import math
import jax
import jax.numpy as jnp
from jax import lax

QH = 64
KVH = 8
HD = 128
D = 8192
BLOCK = 64
SEQ = 6144


def paired_draw(key):
    base = jax.random.fold_in(key, 7)
    key_query, key_keys = jax.random.split(base, 2)
    query_draw = jnp.clip(jax.random.normal(key_query, (SEQ, QH * HD), jnp.float32), -6.0, 6.0) * 1.25
    key_draw = jnp.clip(jax.random.normal(key_keys, (SEQ, KVH * HD), jnp.float32), -6.0, 6.0)
    return (query_draw, key_draw)


def draw_queries(key, part):
    return paired_draw(key)[0].astype(jnp.bfloat16)


def draw_key_rows(key, part):
    return paired_draw(key)[1].astype(jnp.bfloat16)


def draw_block_flags(key, part):
    count = SEQ // BLOCK
    coins = jax.random.randint(jax.random.fold_in(key, 3), (count, count), 0, 2)
    row_ids = jnp.arange(count)[:, None]
    col_ids = jnp.arange(count)[None, :]
    return (jnp.where(col_ids < row_ids, coins, 0) + (col_ids == row_ids).astype(jnp.int32)).astype(jnp.int32)


def levels(rng, shape, cuts, low, top_value):
    def one(axis_at, blocks):
        steps = jax.random.uniform(jax.random.fold_in(jax.random.fold_in(rng, 6), axis_at), (blocks,), jnp.float32, low / len(cuts), top_value / len(cuts))
        return jnp.repeat(jnp.exp(steps), shape[axis_at] // blocks).reshape((-1,) + (1,) * (len(shape) - axis_at - 1))

    loudness = one(*cuts[0])
    for cut in cuts[1:]:
        loudness = loudness * one(*cut)
    return loudness


def scatter_about(stream_key, dims, deviation, bound, pieces=(), held_as=jnp.bfloat16):
    array = deviation * jax.random.normal(stream_key, dims, jnp.float32)
    if pieces:
        array = array * levels(stream_key, dims, pieces, -0.22, 0.18)
    return jnp.clip(array, -bound, bound).astype(held_as)


def setup_inputs(seed: int = 0) -> dict:
    splits = jax.random.split(jax.random.key(seed), 6)
    queries = draw_queries(jax.random.fold_in(splits[5], 71), 0)
    key_rows = draw_key_rows(jax.random.fold_in(splits[5], 71), 0)
    value_rows = scatter_about(splits[2], (SEQ, KVH * HD), 1.0, 6.0, ((0, 48),))
    block_flags = draw_block_flags(jax.random.fold_in(splits[5], 71), 0)
    out_weight = scatter_about(splits[4], (QH * HD, D), (QH * HD // 4) ** -0.5, 0.125, ((0, 16),))
    return dict(queries=queries, key_rows=key_rows, value_rows=value_rows, block_flags=block_flags, out_weight=out_weight)


def reference(queries, key_rows, value_rows, block_flags, out_weight):
    group = QH // KVH
    query_heads = queries.reshape(SEQ, QH, HD)
    key_heads = key_rows.reshape(SEQ, KVH, HD)
    value_heads = value_rows.reshape(SEQ, KVH, HD)
    positions = jnp.arange(SEQ, dtype=jnp.int32)
    expanded = jnp.repeat(jnp.repeat(block_flags, BLOCK, axis=0), BLOCK, axis=1)
    allowed = (expanded == 1) & (positions[None, :] <= positions[:, None])
    scale_factor = 1.0 / math.sqrt(HD)

    def one_head(head_index):
        query_one = lax.dynamic_index_in_dim(query_heads, head_index, 1, keepdims=False)
        key_one = lax.dynamic_index_in_dim(key_heads, head_index // group, 1, keepdims=False)
        value_one = lax.dynamic_index_in_dim(value_heads, head_index // group, 1, keepdims=False)
        scores = jnp.dot(query_one, key_one.T, preferred_element_type=jnp.float32) * scale_factor
        scores = jnp.where(allowed, scores, -jnp.inf)
        row_max = lax.optimization_barrier(jnp.max(scores, axis=1, keepdims=True))
        weights = jnp.exp(scores - row_max)
        totals = lax.optimization_barrier(jnp.sum(weights, axis=1, keepdims=True))
        mixed = jnp.dot(weights.astype(jnp.bfloat16), value_one, preferred_element_type=jnp.float32) / totals
        return mixed.astype(jnp.bfloat16)
    per_head = lax.map(one_head, jnp.arange(QH, dtype=jnp.int32))
    attended = jnp.transpose(per_head, (1, 0, 2)).reshape(SEQ, QH * HD)
    return jnp.dot(attended, out_weight, preferred_element_type=jnp.float32).astype(jnp.bfloat16)
```

```python
import math

import jax
import jax.numpy as jnp
from jax import lax
from jax.experimental import pallas as pl
from jax.experimental.pallas import tpu as pltpu
from jax.sharding import PartitionSpec as P

MESH = pl.DeviceIdType.MESH
HD = 128
TOK = 128
HALF = 64
NZ = 12
NX = 4
NR = 4
COLS = 4096
CW = 512
NC = COLS // CW
SCALE = math.log2(math.e) / math.sqrt(HD)
NEG = 1e30
FLOOR = -1e20
F32 = jnp.float32
BF16 = jnp.bfloat16


def kernel(
    q_ref, k_ref, v_ref, flags, w_ref, out_ref,
    kv, oth, qall, qt, vt, acc, racc, a2, wv, sbuf, own, r1, r1x, s2a, s2b, s2d, f0, f1, own2,
    lsem, wsem, ytx, yrx, tx, rx, qsem, wrem, atx, arx, t1, q1, t2, q2, t3, q3,
):
    c = lax.axis_index("ctx")
    h = lax.axis_index("head")
    r, z = lax.div(c, NZ), lax.rem(c, NZ)
    x, yl, co = lax.div(h, 4), lax.rem(lax.div(h, 2), 2), lax.rem(h, 2)
    sg = 1 - 2 * yl

    def dev(rr, zz, xx, yy, cc):
        return {"ctx": rr * NZ + zz, "head": xx * 4 + yy * 2 + cc}

    zp = dev(r, lax.rem(z + 1, NZ), x, yl, co)
    zm = dev(r, lax.rem(z + NZ - 1, NZ), x, yl, co)
    r_minus, r_plus, r_far = lax.rem(r - sg + NR, NR), lax.rem(r + sg + NR, NR), lax.rem(r + 2, NR)
    dev_a = dev(r_minus, z, x, 1 - yl, co)
    dev_b = dev(r_minus, z, x, yl, co)
    dev_b_src = dev(r_plus, z, x, yl, co)
    dev_c = dev(r_far, z, x, 1 - yl, co)
    mate = dev(r, z, x, yl, 1 - co)

    def xdev(d, cc):
        return dev(r, z, lax.rem(x + d, NX), yl, cc)

    def ydev(cc):
        return dev(r, z, x, 1 - yl, cc)

    row_of = (r, r_minus, r_plus, r_far)

    head_own = x * 2 + yl
    head_oth = x * 2 + 1 - yl
    rows = pl.ds(pl.multiple_of(co * HALF, HALF), HALF)

    def head_cols(kvh):
        return pl.ds(pl.multiple_of(kvh * HD, HD), HD)

    loads = [
        pltpu.make_async_copy(k_ref.at[rows, head_cols(head_own)], kv.at[z, 0, :, pl.ds(0, HD)], lsem.at[0]),
        pltpu.make_async_copy(v_ref.at[rows, head_cols(head_own)], kv.at[z, 0, :, pl.ds(HD, HD)], lsem.at[1]),
        pltpu.make_async_copy(k_ref.at[rows, head_cols(head_oth)], oth.at[:, pl.ds(0, HD)], lsem.at[2]),
        pltpu.make_async_copy(v_ref.at[rows, head_cols(head_oth)], oth.at[:, pl.ds(HD, HD)], lsem.at[3]),
        pltpu.make_async_copy(q_ref, qall.at[co], lsem.at[4]),
    ]
    for copy in loads:
        copy.start()
    w_own = pltpu.make_async_copy(
        w_ref.at[:, pl.ds(pl.multiple_of(co * COLS, COLS), COLS)], wv.at[co], wsem
    )
    w_own.start()

    barrier = pltpu.get_barrier_semaphore()
    peers = [zp, zm, dev_a, dev_b_src, dev_c, mate, ydev(0), ydev(1)]
    peers += [xdev(d, cc) for d in (1, 2, 3) for cc in (0, 1)]
    for peer in peers:
        pl.semaphore_signal(barrier, inc=1, device_id=peer, device_id_type=MESH)
    pl.semaphore_wait(barrier, len(peers))

    def remote(src, dst, send_sem, recv_sem, peer):
        return pltpu.make_async_remote_copy(
            src_ref=src, dst_ref=dst, send_sem=send_sem, recv_sem=recv_sem, device_id=peer, device_id_type=MESH
        )

    def at_plus(d):
        return lax.rem(z + NZ - d, NZ)

    def at_minus(d):
        return lax.rem(z + d, NZ)

    def hop(way, d, j):
        zi = at_plus(d) if way == 0 else at_minus(d)
        return remote(kv.at[zi, j], kv.at[zi, j], tx.at[way, d, j], rx.at[way, d, j], zp if way == 0 else zm)

    def arrival(way, d, j):
        zi = at_plus(d) if way == 0 else at_minus(d)
        return remote(kv.at[zi, j], kv.at[zi, j], tx.at[way, d - 1, j], rx.at[way, d - 1, j], zp if way == 0 else zm)

    for copy in loads[:2]:
        copy.wait()
    hop(0, 0, 0).start()
    hop(1, 0, 0).start()
    for copy in loads[2:4]:
        copy.wait()
    y_copies = [
        remote(oth, kv.at[z, 1], ytx.at[0], yrx.at[0], dev_a),
        remote(kv.at[z, 0], kv.at[z, 2], ytx.at[1], yrx.at[1], dev_b),
        remote(oth, kv.at[z, 3], ytx.at[2], yrx.at[2], dev_c),
    ]
    for copy in y_copies:
        copy.start()
    q_copy = remote(q_ref, qall.at[co], qsem.at[0], qsem.at[1], mate)
    q_copy.start()
    w_copy = remote(
        w_ref.at[:, pl.ds(pl.multiple_of((1 - co) * COLS, COLS), COLS)], wv.at[co], wrem.at[0], wrem.at[1], mate
    )
    w_copy.start()

    lane = lax.broadcasted_iota(jnp.int32, (1, 2 * TOK), 1)
    first_half = lax.rem(lane, TOK) < HALF

    loads[4].wait()
    q_copy.wait_recv()
    for i in range(8):
        qt[i] = qall[i // 4, :, (i % 4) * HD : (i % 4 + 1) * HD].T
    for g in range(4):
        acc[g, :HD] = jnp.zeros((HD, 2 * TOK), F32)
        acc[g, HD : HD + 8] = jnp.where(
            lax.broadcasted_iota(jnp.int32, (8, 2 * TOK), 0) == 0, FLOOR, 0.0
        )

    for j in (1, 2, 3):
        y_copies[j - 1].wait_recv()
        hop(0, 0, j).start()
        hop(1, 0, j).start()

    def prepare(slot, zi):
        vt[slot] = kv[zi, :, :, HD:].reshape(4 * HALF, HD).T

    def item(slot, zi, g, diagonal=False):
        keys = kv[zi, :, :, :HD].reshape(4 * HALF, HD)
        query = jnp.concatenate([qt[2 * g], qt[2 * g + 1]], axis=1)
        scores = jnp.dot(keys, query, preferred_element_type=F32)
        parts = []
        for j in range(4):
            at = 2 * (row_of[j] * NZ + zi) + co
            flag = jnp.where(first_half, flags[0, at], flags[1, at]).astype(F32)
            bias = (flag - 1.0) * NEG
            if diagonal and j == 0:
                key_pos = co * HALF + lax.broadcasted_iota(jnp.int32, (HALF, 2 * TOK), 0)
                query_pos = lax.rem(lax.broadcasted_iota(jnp.int32, (HALF, 2 * TOK), 1), TOK)
                bias = jnp.where(key_pos <= query_pos, bias, -NEG)
            parts.append(scores[j * HALF : (j + 1) * HALF] * SCALE + bias)
        scores = jnp.concatenate(parts, axis=0)
        old = acc[g, HD : HD + 1]
        new = jnp.maximum(old, jnp.max(scores, axis=0, keepdims=True))
        weights = jnp.exp2(scores - new)
        factor = jnp.exp2(old - new)
        acc[g, HD : HD + 1] = new
        acc[g, HD + 1 : HD + 2] = acc[g, HD + 1 : HD + 2] * factor + jnp.sum(weights, axis=0, keepdims=True)
        acc[g, :HD] = acc[g, :HD] * factor + jnp.dot(vt[slot], weights.astype(BF16), preferred_element_type=F32)

    for j in range(4):
        arrival(0, 1, j).wait_recv()
        hop(0, 1, j).start()
        arrival(1, 1, j).wait_recv()
        hop(1, 1, j).start()
        if j == 0:
            prepare(0, z)
        item(0, z, j, diagonal=True)

    def step(d, carry):
        for j in range(4):
            for way in (0, 1):
                late = (j < 2) == (way == 0)
                if late:
                    arrival(way, d, j).wait_recv()

                    @pl.when(d < 6)
                    def _():
                        hop(way, d, j).start()
                else:

                    @pl.when(d < 6)
                    def _():
                        arrival(way, d, j).wait_recv()

                    @pl.when(d < 5)
                    def _():
                        hop(way, d, j).start()

            if j == 0:
                prepare(0, at_plus(d - 1))
                prepare(1, at_minus(d - 1))
            item(0, at_plus(d - 1), j)
            item(1, at_minus(d - 1), j)
        return carry

    lax.fori_loop(2, 7, step, 0)

    a_copies = [remote(acc.at[g], racc.at[g], atx.at[g], arx.at[g], mate) for g in range(4)]
    prepare(0, at_minus(6))
    for g in range(4):
        item(0, at_minus(6), g)
        a_copies[g].start()

    def place(xx, yy):
        dx = lax.rem(xx - x + NX + 3, NX)
        near = lax.rem(yy + yl, 2)
        by_y = dx + 4 * (1 - near)
        by_x = dx * 2 + near
        return jnp.where(co == 0, by_y, by_x)

    for g in range(4):
        a_copies[g].wait_recv()
        m0, m1 = acc[g, HD : HD + 1], racc[g, HD : HD + 1]
        top = jnp.maximum(m0, m1)
        e0, e1 = jnp.exp2(m0 - top), jnp.exp2(m1 - top)
        total = acc[g, HD + 1 : HD + 2] * e0 + racc[g, HD + 1 : HD + 2] * e1
        mixed = (acc[g, :HD] * e0 + racc[g, :HD] * e1) / total
        for i in (0, 1):
            tile = mixed[:, i * TOK : (i + 1) * TOK].T.astype(BF16)
            cols = slice((2 * g + i) * HD, (2 * g + i + 1) * HD)
            for xx in range(4):
                for yy in range(2):
                    at = (xx * 2 + yy) * 16
                    a2[place(xx, yy), :, cols] = tile[at : at + 16]

    w_own.wait()
    w_copy.wait_recv()

    def send1y(n):
        return remote(sbuf.at[n, pl.ds(0, 64)], r1.at[n], t1.at[0, n], q1.at[0, n], ydev(0))

    def send1x(n, d):
        return remote(
            sbuf.at[n, pl.ds(32 * (d - 1), 32)], r1x.at[d - 1, n], t1.at[d - 1, n], q1.at[d - 1, n], xdev(d, 1)
        )

    def project(n, carry):
        cols = pl.ds(pl.multiple_of(n * CW, CW), CW)
        part = jnp.dot(
            a2[...].reshape(TOK, 8 * HD), wv[:, :, cols].reshape(8 * HD, CW), preferred_element_type=F32
        )
        sbuf[n] = part[:96].astype(BF16)
        own[n] = part[64:]

        @pl.when(co == 0)
        def _():
            send1y(n).start()

        @pl.when(co == 1)
        def _():
            for d in (2, 1, 3):
                send1x(n, d).start()

        return carry

    lax.fori_loop(0, NC, project, 0)

    def send2x(n, d, cc):
        return remote(s2a.at[n, d - 1, cc], f0.at[d - 1, n], t2.at[d - 1, cc, n], q2.at[d - 1, n], xdev(d, cc))

    def send2y(n, cc):
        return remote(s2b.at[n, cc], f1.at[0, n], t2.at[0, cc, n], q2.at[3, n], ydev(cc))

    def send3a(n):
        return remote(s2d.at[n], f0.at[3, n], t3.at[n], q3.at[n], mate)

    def send3b(n):
        return remote(s2d.at[n], f1.at[1, n], t3.at[n], q3.at[n], mate)

    @pl.when(co == 0)
    def _():
        def second(n, carry):
            send1y(n).wait_recv()
            total = own[n] + r1[n].astype(F32)
            for d in (2, 1, 3):
                for cc in (0, 1):
                    at = 16 * (d - 1) + 8 * cc
                    s2a[n, d - 1, cc] = total[at : at + 8].astype(BF16)
                    send2x(n, d, cc).start()
            own2[n] = total[48:56]
            s2d[n] = total[56:].astype(BF16)
            send3a(n).start()
            return carry

        lax.fori_loop(0, NC, second, 0)

        def last(n, carry):
            for d in (1, 2, 3):
                send2x(n, d, 0).wait_recv()
            total = own2[n] + f0[0, n].astype(F32) + f0[1, n].astype(F32) + f0[2, n].astype(F32)
            out_ref[:, pl.ds(pl.multiple_of(n * CW, CW), CW)] = total.astype(BF16)
            send2y(n, 0).wait_recv()
            send3b(n).wait_recv()
            total = f1[0, n].astype(F32) + f1[1, n].astype(F32)
            out_ref[:, pl.ds(pl.multiple_of(COLS + n * CW, CW), CW)] = total.astype(BF16)
            return carry

        lax.fori_loop(0, NC, last, 0)

        def sent(n, carry):
            send1y(n).wait_send()
            for d in (1, 2, 3):
                for cc in (0, 1):
                    send2x(n, d, cc).wait_send()
            send3a(n).wait_send()
            return carry

        lax.fori_loop(0, NC, sent, 0)

    @pl.when(co == 1)
    def _():
        def second(n, carry):
            for d in (1, 2, 3):
                send1x(n, d).wait_recv()
            total = own[n, pl.ds(32, 32)]
            for d in range(3):
                total = total + r1x[d, n].astype(F32)
            for cc in (0, 1):
                s2b[n, cc] = total[16 + 8 * cc : 24 + 8 * cc].astype(BF16)
                send2y(n, cc).start()
            s2d[n] = total[:8].astype(BF16)
            send3b(n).start()
            own2[n] = total[8:16]
            return carry

        lax.fori_loop(0, NC, second, 0)

        def last(n, carry):
            for d in (1, 2, 3):
                send2x(n, d, 1).wait_recv()
            send3a(n).wait_recv()
            total = f0[3, n].astype(F32) + f0[0, n].astype(F32) + f0[1, n].astype(F32) + f0[2, n].astype(F32)
            out_ref[:, pl.ds(pl.multiple_of(n * CW, CW), CW)] = total.astype(BF16)
            send2y(n, 1).wait_recv()
            total = own2[n] + f1[0, n].astype(F32)
            out_ref[:, pl.ds(pl.multiple_of(COLS + n * CW, CW), CW)] = total.astype(BF16)
            return carry

        lax.fori_loop(0, NC, last, 0)

        def sent(n, carry):
            for d in (1, 2, 3):
                send1x(n, d).wait_send()
            for cc in (0, 1):
                send2y(n, cc).wait_send()
            send3b(n).wait_send()
            return carry

        lax.fori_loop(0, NC, sent, 0)

    for copy in y_copies + [q_copy, w_copy] + a_copies:
        copy.wait_send()

    def drain(d, carry):
        for j in range(4):
            for way in (0, 1):
                if (j < 2) == (way == 0):
                    hop(way, d, j).wait_send()
                else:

                    @pl.when(d < 5)
                    def _():
                        hop(way, d, j).wait_send()

        return carry

    lax.fori_loop(0, 6, drain, 0)


def local(queries, key_rows, value_rows, block_flags, out_weight):
    dma = pltpu.SemaphoreType.DMA
    hbm = pl.BlockSpec(memory_space=pl.ANY)
    vmem = pltpu.VMEM
    return pl.pallas_call(
        kernel,
        out_shape=jax.ShapeDtypeStruct((8, 2 * COLS), BF16),
        in_specs=[hbm, hbm, hbm, pl.BlockSpec(memory_space=pltpu.SMEM), hbm],
        out_specs=pl.BlockSpec(memory_space=pltpu.VMEM),
        scratch_shapes=[
            vmem((NZ, 4, HALF, 2 * HD), BF16),
            vmem((HALF, 2 * HD), BF16),
            vmem((2, TOK, 4 * HD), BF16),
            vmem((8, HD, TOK), BF16),
            vmem((2, HD, 4 * HALF), BF16),
            vmem((4, HD + 8, 2 * TOK), F32),
            vmem((4, HD + 8, 2 * TOK), F32),
            vmem((8, 16, 8 * HD), BF16),
            vmem((2, 4 * HD, COLS), BF16),
            vmem((NC, 96, CW), BF16),
            vmem((NC, 64, CW), F32),
            vmem((NC, 64, CW), BF16),
            vmem((3, NC, 32, CW), BF16),
            vmem((NC, 3, 2, 8, CW), BF16),
            vmem((NC, 2, 8, CW), BF16),
            vmem((NC, 8, CW), BF16),
            vmem((4, NC, 8, CW), BF16),
            vmem((2, NC, 8, CW), BF16),
            vmem((NC, 8, CW), F32),
            dma((5,)),
            dma,
            dma((3,)),
            dma((3,)),
            dma((2, 6, 4)),
            dma((2, 6, 4)),
            dma((2,)),
            dma((2,)),
            dma((4,)),
            dma((4,)),
            dma((3, NC)),
            dma((3, NC)),
            dma((3, 2, NC)),
            dma((4, NC)),
            dma((NC,)),
            dma((NC,)),
        ],
        compiler_params=pltpu.CompilerParams(
            collective_id=0, has_side_effects=True, vmem_limit_bytes=60 * 2**20
        ),
        name="attention_layer",
    )(queries, key_rows, value_rows, block_flags, out_weight)


def solution(mesh):
    placed = (P("ctx", "head"), P("ctx", None), P("ctx", None), P("ctx", None), P("head", None))
    return jax.shard_map(
        local, mesh=mesh, in_specs=placed, out_specs=P(("ctx", "head"), None), check_vma=False
    )
```

```python
import math

import jax
import jax.numpy as jnp
from jax import lax
from jax.experimental import pallas as pl
from jax.experimental.pallas import tpu as pltpu
from jax.sharding import PartitionSpec as P

MESH = pl.DeviceIdType.MESH
HD = 128
TOK = 128
HALF = 64
NZ = 12
NX = 4
NR = 4
COLS = 4096
CW = 512
NC = COLS // CW
SCALE = math.log2(math.e) / math.sqrt(HD)
NEG = 1e30
FLOOR = -1e20
F32 = jnp.float32
BF16 = jnp.bfloat16


def kernel(
    q_ref, k_ref, v_ref, flags_ref, w_ref, out_ref,
    flags, obuf, kv, oth, qall, qt, vt, acc, racc, a2, wv, sbuf, own, r1, r1x, s2a, s2b, s2d, f0, f1, own2,
    lsem, wsem, fsem, osem, ytx, yrx, tx, rx, qsem, wrem, atx, arx, t1, q1, t2, q2, t3, q3,
):
    c = lax.axis_index("ctx")
    h = lax.axis_index("head")
    r, z = lax.div(c, NZ), lax.rem(c, NZ)
    x, yl, co = lax.div(h, 4), lax.rem(lax.div(h, 2), 2), lax.rem(h, 2)
    sg = 1 - 2 * yl

    def dev(rr, zz, xx, yy, cc):
        return {"ctx": rr * NZ + zz, "head": xx * 4 + yy * 2 + cc}

    zp = dev(r, lax.rem(z + 1, NZ), x, yl, co)
    zm = dev(r, lax.rem(z + NZ - 1, NZ), x, yl, co)
    r_minus, r_plus, r_far = lax.rem(r - sg + NR, NR), lax.rem(r + sg + NR, NR), lax.rem(r + 2, NR)
    dev_a = dev(r_minus, z, x, 1 - yl, co)
    dev_b = dev(r_minus, z, x, yl, co)
    dev_b_src = dev(r_plus, z, x, yl, co)
    dev_c = dev(r_far, z, x, 1 - yl, co)
    mate = dev(r, z, x, yl, 1 - co)

    def xdev(d, cc):
        return dev(r, z, lax.rem(x + d, NX), yl, cc)

    def ydev(cc):
        return dev(r, z, x, 1 - yl, cc)

    row_of = (r, r_minus, r_plus, r_far)

    head_own = x * 2 + yl
    head_oth = x * 2 + 1 - yl
    rows = pl.ds(pl.multiple_of(co * HALF, HALF), HALF)

    def head_cols(kvh):
        return pl.ds(pl.multiple_of(kvh * HD, HD), HD)

    loads = [
        pltpu.make_async_copy(k_ref.at[rows, head_cols(head_own)], kv.at[z, 0, :, pl.ds(0, HD)], lsem.at[0]),
        pltpu.make_async_copy(v_ref.at[rows, head_cols(head_own)], kv.at[z, 0, :, pl.ds(HD, HD)], lsem.at[1]),
        pltpu.make_async_copy(k_ref.at[rows, head_cols(head_oth)], oth.at[:, pl.ds(0, HD)], lsem.at[2]),
        pltpu.make_async_copy(v_ref.at[rows, head_cols(head_oth)], oth.at[:, pl.ds(HD, HD)], lsem.at[3]),
        pltpu.make_async_copy(q_ref, qall.at[co], lsem.at[4]),
    ]
    for copy in loads:
        copy.start()
    flag_load = pltpu.make_async_copy(flags_ref, flags, fsem)
    flag_load.start()
    w_own = pltpu.make_async_copy(
        w_ref.at[:, pl.ds(pl.multiple_of(co * COLS, COLS), COLS)], wv.at[co], wsem
    )
    w_own.start()

    barrier = pltpu.get_barrier_semaphore()
    peers = [zp, zm, dev_a, dev_b_src, dev_c, mate, ydev(0), ydev(1)]
    peers += [xdev(d, cc) for d in (1, 2, 3) for cc in (0, 1)]
    for peer in peers:
        pl.semaphore_signal(barrier, inc=1, device_id=peer, device_id_type=MESH)
    pl.semaphore_wait(barrier, len(peers))

    def remote(src, dst, send_sem, recv_sem, peer):
        return pltpu.make_async_remote_copy(
            src_ref=src, dst_ref=dst, send_sem=send_sem, recv_sem=recv_sem, device_id=peer, device_id_type=MESH
        )

    def at_plus(d):
        return lax.rem(z + NZ - d, NZ)

    def at_minus(d):
        return lax.rem(z + d, NZ)

    def hop(way, d, j):
        zi = at_plus(d) if way == 0 else at_minus(d)
        return remote(kv.at[zi, j], kv.at[zi, j], tx.at[way, d, j], rx.at[way, d, j], zp if way == 0 else zm)

    def arrival(way, d, j):
        zi = at_plus(d) if way == 0 else at_minus(d)
        return remote(kv.at[zi, j], kv.at[zi, j], tx.at[way, d - 1, j], rx.at[way, d - 1, j], zp if way == 0 else zm)

    for copy in loads[:2]:
        copy.wait()
    hop(0, 0, 0).start()
    hop(1, 0, 0).start()
    for copy in loads[2:4]:
        copy.wait()
    y_copies = [
        remote(oth, kv.at[z, 1], ytx.at[0], yrx.at[0], dev_a),
        remote(kv.at[z, 0], kv.at[z, 2], ytx.at[1], yrx.at[1], dev_b),
        remote(oth, kv.at[z, 3], ytx.at[2], yrx.at[2], dev_c),
    ]
    for copy in reversed(y_copies):
        copy.start()
    q_copy = remote(q_ref, qall.at[co], qsem.at[0], qsem.at[1], mate)
    q_copy.start()
    w_copy = remote(
        w_ref.at[:, pl.ds(pl.multiple_of((1 - co) * COLS, COLS), COLS)], wv.at[co], wrem.at[0], wrem.at[1], mate
    )
    w_copy.start()

    lane = lax.broadcasted_iota(jnp.int32, (1, 2 * TOK), 1)
    first_half = lax.rem(lane, TOK) < HALF

    loads[4].wait()
    q_copy.wait_recv()
    for i in range(8):
        side = slice((i % 2) * TOK, (i % 2 + 1) * TOK)
        qt[i // 2, :, side] = qall[i // 4, :, (i % 4) * HD : (i % 4 + 1) * HD].T
    for g in range(4):
        acc[g, :HD] = jnp.zeros((HD, 2 * TOK), F32)
        acc[g, HD : HD + 8] = jnp.where(
            lax.broadcasted_iota(jnp.int32, (8, 2 * TOK), 0) == 0, FLOOR, 0.0
        )

    def relay(way, d, j):
        last = 6 if (j < 2) == (way == 0) else 5

        def go():
            arrival(way, d, j).wait_recv()

        def on():
            hop(way, d, j).start()

        if isinstance(d, int):
            if d <= last:
                go()
            if d < last:
                on()
        else:
            pl.when(d <= last)(go)
            pl.when(d < last)(on)

    for way in (0, 1):
        relay(way, 1, 0)
    for j in (1, 2, 3):
        y_copies[j - 1].wait_recv()
        hop(0, 0, j).start()
        hop(1, 0, j).start()
    flag_load.wait()
    def prepare(slot, zi):
        vt[slot] = kv[zi, :, :, HD:].reshape(4 * HALF, HD).T

    def attend(bundles, g, diagonal=False):
        query = qt[g]
        old = acc[g, HD : HD + 1]
        new = old
        tiles = []
        for slot, zi in bundles:
            keys = kv[zi, :, :, :HD].reshape(4 * HALF, HD)
            scores = jnp.dot(keys, query, preferred_element_type=F32)
            parts = []
            for j in range(4):
                at = 2 * (row_of[j] * NZ + zi) + co
                flag = jnp.where(first_half, flags[0, at], flags[1, at]).astype(F32)
                bias = (flag - 1.0) * NEG
                if diagonal and j == 0:
                    key_pos = co * HALF + lax.broadcasted_iota(jnp.int32, (HALF, 2 * TOK), 0)
                    query_pos = lax.rem(lax.broadcasted_iota(jnp.int32, (HALF, 2 * TOK), 1), TOK)
                    bias = jnp.where(key_pos <= query_pos, bias, -NEG)
                parts.append(scores[j * HALF : (j + 1) * HALF] * SCALE + bias)
            scores = jnp.concatenate(parts, axis=0)
            new = jnp.maximum(new, jnp.max(scores, axis=0, keepdims=True))
            tiles.append(scores)
        factor = jnp.exp2(old - new)
        total = acc[g, HD + 1 : HD + 2] * factor
        mixed = acc[g, :HD] * factor
        for (slot, _), scores in zip(bundles, tiles):
            weights = jnp.exp2(scores - new)
            total = total + jnp.sum(weights, axis=0, keepdims=True)
            mixed = mixed + jnp.dot(vt[slot], weights.astype(BF16), preferred_element_type=F32)
        acc[g, HD : HD + 1] = new
        acc[g, HD + 1 : HD + 2] = total
        acc[g, :HD] = mixed

    def relays(k, j):
        for way in (0, 1):
            relay(way, k + 1 if j == 0 else k, j)

    for j in range(4):
        relays(1, j)
        if j == 0:
            prepare(0, z)
        attend([(0, z)], j, diagonal=True)

    def step(k, carry):
        for j in range(4):
            relays(k, j)
            if j == 0:
                prepare(0, at_plus(k - 1))
                prepare(1, at_minus(k - 1))
            attend([(0, at_plus(k - 1)), (1, at_minus(k - 1))], j)
        return carry

    lax.fori_loop(2, 7, step, 0)

    a_copies = [remote(acc.at[g], racc.at[g], atx.at[g], arx.at[g], mate) for g in range(4)]
    prepare(0, at_minus(6))
    for g in range(4):
        attend([(0, at_minus(6))], g)
        a_copies[g].start()

    def place(xx, yy):
        dx = lax.rem(xx - x + NX + 3, NX)
        near = lax.rem(yy + yl, 2)
        by_y = dx + 4 * (1 - near)
        by_x = dx * 2 + near
        return jnp.where(co == 0, by_y, by_x)

    for g in range(4):
        a_copies[g].wait_recv()
        m0, m1 = acc[g, HD : HD + 1], racc[g, HD : HD + 1]
        top = jnp.maximum(m0, m1)
        e0, e1 = jnp.exp2(m0 - top), jnp.exp2(m1 - top)
        total = acc[g, HD + 1 : HD + 2] * e0 + racc[g, HD + 1 : HD + 2] * e1
        mixed = (acc[g, :HD] * e0 + racc[g, :HD] * e1) / total
        for i in (0, 1):
            tile = mixed[:, i * TOK : (i + 1) * TOK].T.astype(BF16)
            cols = slice((2 * g + i) * HD, (2 * g + i + 1) * HD)
            for xx in range(4):
                for yy in range(2):
                    at = (xx * 2 + yy) * 16
                    a2[place(xx, yy), :, cols] = tile[at : at + 16]

    w_own.wait()
    w_copy.wait_recv()

    def send1y(n):
        return remote(sbuf.at[n, pl.ds(0, 64)], r1.at[n], t1.at[0, n], q1.at[0, n], ydev(0))

    def send1x(n, d):
        return remote(
            sbuf.at[n, pl.ds(32 * (d - 1), 32)], r1x.at[d - 1, n], t1.at[d - 1, n], q1.at[d - 1, n], xdev(d, 1)
        )

    def project(n, carry):
        cols = pl.ds(pl.multiple_of(n * CW, CW), CW)
        part = jnp.dot(
            a2[...].reshape(TOK, 8 * HD), wv[:, :, cols].reshape(8 * HD, CW), preferred_element_type=F32
        )
        sbuf[n] = part[:96].astype(BF16)
        own[n] = part[64:]

        @pl.when(co == 0)
        def _():
            send1y(n).start()

        @pl.when(co == 1)
        def _():
            for d in (2, 1, 3):
                send1x(n, d).start()

        return carry

    lax.fori_loop(0, NC, project, 0)

    def send2x(n, d, cc):
        return remote(s2a.at[n, d - 1, cc], f0.at[d - 1, n], t2.at[d - 1, cc, n], q2.at[d - 1, n], xdev(d, cc))

    def send2y(n, cc):
        return remote(s2b.at[n, cc], f1.at[0, n], t2.at[0, cc, n], q2.at[3, n], ydev(cc))

    def put(side, n):
        at = pl.multiple_of(side * COLS + n * CW, CW)
        return pltpu.make_async_copy(obuf.at[side, n], out_ref.at[:, pl.ds(at, CW)], osem.at[side, n])

    def send3a(n):
        return remote(s2d.at[n], f0.at[3, n], t3.at[n], q3.at[n], mate)

    def send3b(n):
        return remote(s2d.at[n], f1.at[1, n], t3.at[n], q3.at[n], mate)

    @pl.when(co == 0)
    def _():
        def second(n, carry):
            send1y(n).wait_recv()
            total = own[n] + r1[n].astype(F32)
            for d in (2, 1, 3):
                for cc in (0, 1):
                    at = 16 * (d - 1) + 8 * cc
                    s2a[n, d - 1, cc] = total[at : at + 8].astype(BF16)
                    send2x(n, d, cc).start()
            own2[n] = total[48:56]
            s2d[n] = total[56:].astype(BF16)
            send3a(n).start()
            return carry

        lax.fori_loop(0, NC, second, 0)

        def last(n, carry):
            for d in (1, 2, 3):
                send2x(n, d, 0).wait_recv()
            total = own2[n] + f0[0, n].astype(F32) + f0[1, n].astype(F32) + f0[2, n].astype(F32)
            obuf[0, n] = total.astype(BF16)
            put(0, n).start()
            send2y(n, 0).wait_recv()
            send3b(n).wait_recv()
            total = f1[0, n].astype(F32) + f1[1, n].astype(F32)
            obuf[1, n] = total.astype(BF16)
            put(1, n).start()
            return carry

        lax.fori_loop(0, NC, last, 0)

        def sent(n, carry):
            send1y(n).wait_send()
            for d in (1, 2, 3):
                for cc in (0, 1):
                    send2x(n, d, cc).wait_send()
            send3a(n).wait_send()
            return carry

        lax.fori_loop(0, NC, sent, 0)

    @pl.when(co == 1)
    def _():
        def second(n, carry):
            for d in (1, 2, 3):
                send1x(n, d).wait_recv()
            total = own[n, pl.ds(32, 32)]
            for d in range(3):
                total = total + r1x[d, n].astype(F32)
            for cc in (0, 1):
                s2b[n, cc] = total[16 + 8 * cc : 24 + 8 * cc].astype(BF16)
                send2y(n, cc).start()
            s2d[n] = total[:8].astype(BF16)
            send3b(n).start()
            own2[n] = total[8:16]
            return carry

        lax.fori_loop(0, NC, second, 0)

        def last(n, carry):
            for d in (1, 2, 3):
                send2x(n, d, 1).wait_recv()
            send3a(n).wait_recv()
            total = f0[3, n].astype(F32) + f0[0, n].astype(F32) + f0[1, n].astype(F32) + f0[2, n].astype(F32)
            obuf[0, n] = total.astype(BF16)
            put(0, n).start()
            send2y(n, 1).wait_recv()
            total = own2[n] + f1[0, n].astype(F32)
            obuf[1, n] = total.astype(BF16)
            put(1, n).start()
            return carry

        lax.fori_loop(0, NC, last, 0)

        def sent(n, carry):
            for d in (1, 2, 3):
                send1x(n, d).wait_send()
            for cc in (0, 1):
                send2y(n, cc).wait_send()
            send3b(n).wait_send()
            return carry

        lax.fori_loop(0, NC, sent, 0)

    def stored(n, carry):
        for side in (0, 1):
            put(side, n).wait()
        return carry

    lax.fori_loop(0, NC, stored, 0)

    for copy in y_copies + [q_copy, w_copy] + a_copies:
        copy.wait_send()

    def drain(d, carry):
        for j in range(4):
            for way in (0, 1):
                if (j < 2) == (way == 0):
                    hop(way, d, j).wait_send()
                else:

                    @pl.when(d < 5)
                    def _():
                        hop(way, d, j).wait_send()

        return carry

    lax.fori_loop(0, 6, drain, 0)


def local(queries, key_rows, value_rows, block_flags, out_weight):
    dma = pltpu.SemaphoreType.DMA
    hbm = pl.BlockSpec(memory_space=pl.ANY)
    vmem = pltpu.VMEM
    return pl.pallas_call(
        kernel,
        out_shape=jax.ShapeDtypeStruct((8, 2 * COLS), BF16),
        in_specs=[hbm] * 5,
        out_specs=hbm,
        scratch_shapes=[
            pltpu.SMEM((2, 96), jnp.int32),
            vmem((2, NC, 8, CW), BF16),
            vmem((NZ, 4, HALF, 2 * HD), BF16),
            vmem((HALF, 2 * HD), BF16),
            vmem((2, TOK, 4 * HD), BF16),
            vmem((4, HD, 2 * TOK), BF16),
            vmem((2, HD, 4 * HALF), BF16),
            vmem((4, HD + 8, 2 * TOK), F32),
            vmem((4, HD + 8, 2 * TOK), F32),
            vmem((8, 16, 8 * HD), BF16),
            vmem((2, 4 * HD, COLS), BF16),
            vmem((NC, 96, CW), BF16),
            vmem((NC, 64, CW), F32),
            vmem((NC, 64, CW), BF16),
            vmem((3, NC, 32, CW), BF16),
            vmem((NC, 3, 2, 8, CW), BF16),
            vmem((NC, 2, 8, CW), BF16),
            vmem((NC, 8, CW), BF16),
            vmem((4, NC, 8, CW), BF16),
            vmem((2, NC, 8, CW), BF16),
            vmem((NC, 8, CW), F32),
            dma((5,)),
            dma,
            dma,
            dma((2, NC)),
            dma((3,)),
            dma((3,)),
            dma((2, 6, 4)),
            dma((2, 6, 4)),
            dma((2,)),
            dma((2,)),
            dma((4,)),
            dma((4,)),
            dma((3, NC)),
            dma((3, NC)),
            dma((3, 2, NC)),
            dma((4, NC)),
            dma((NC,)),
            dma((NC,)),
        ],
        compiler_params=pltpu.CompilerParams(
            collective_id=0, has_side_effects=True, vmem_limit_bytes=60 * 2**20
        ),
        name="attention_layer",
    )(queries, key_rows, value_rows, block_flags, out_weight)


def solution(mesh):
    placed = (P("ctx", "head"), P("ctx", None), P("ctx", None), P("ctx", None), P("head", None))
    return jax.shard_map(
        local, mesh=mesh, in_specs=placed, out_specs=P(("ctx", "head"), None), check_vma=False
    )
```

```python
import math

import jax
import jax.numpy as jnp
from jax import lax
from jax.experimental import pallas as pl
from jax.experimental.pallas import tpu as pltpu
from jax.sharding import PartitionSpec as P

MESH = pl.DeviceIdType.MESH
HD = 128
TOK = 128
HALF = 64
NZ = 12
NX = 4
NR = 4
COLS = 4096
CW = 512
NC = COLS // CW
SCALE = math.log2(math.e) / math.sqrt(HD)
NEG = 1e30
FLOOR = -1e20
F32 = jnp.float32
BF16 = jnp.bfloat16


def kernel(
    q_ref, k_ref, v_ref, flags_ref, w_ref, out_ref,
    flags, obuf, kv, oth, qall, qt, vt, acc, racc, a2, wv, sbuf, own, r1, r1x, s2a, s2b, s2d, f0, f1, own2,
    lsem, wsem, fsem, osem, ytx, yrx, tx, rx, qsem, wrem, atx, arx, t1, q1, t2, q2, t3, q3,
):
    c = lax.axis_index("ctx")
    h = lax.axis_index("head")
    r, z = lax.div(c, NZ), lax.rem(c, NZ)
    x, yl, co = lax.div(h, 4), lax.rem(lax.div(h, 2), 2), lax.rem(h, 2)
    sg = 1 - 2 * yl

    def dev(rr, zz, xx, yy, cc):
        return {"ctx": rr * NZ + zz, "head": xx * 4 + yy * 2 + cc}

    def ahead(way, d):
        return lax.rem(z + NZ + (1 - 2 * way) * d, NZ)

    def zdev(way, d):
        return dev(r, ahead(way, d), x, yl, co)

    r_minus, r_plus, r_far = lax.rem(r - sg + NR, NR), lax.rem(r + sg + NR, NR), lax.rem(r + 2, NR)
    dev_a = dev(r_minus, z, x, 1 - yl, co)
    dev_b = dev(r_minus, z, x, yl, co)
    dev_b_src = dev(r_plus, z, x, yl, co)
    dev_c = dev(r_far, z, x, 1 - yl, co)
    mate = dev(r, z, x, yl, 1 - co)

    def xdev(d, cc):
        return dev(r, z, lax.rem(x + d, NX), yl, cc)

    def ydev(cc):
        return dev(r, z, x, 1 - yl, cc)

    row_of = (r, r_minus, r_plus, r_far)

    head_own = x * 2 + yl
    head_oth = x * 2 + 1 - yl
    rows = pl.ds(pl.multiple_of(co * HALF, HALF), HALF)

    def head_cols(kvh):
        return pl.ds(pl.multiple_of(kvh * HD, HD), HD)

    loads = [
        pltpu.make_async_copy(k_ref.at[rows, head_cols(head_own)], kv.at[z, 0, :, pl.ds(0, HD)], lsem.at[0]),
        pltpu.make_async_copy(v_ref.at[rows, head_cols(head_own)], kv.at[z, 0, :, pl.ds(HD, HD)], lsem.at[1]),
        pltpu.make_async_copy(k_ref.at[rows, head_cols(head_oth)], oth.at[:, pl.ds(0, HD)], lsem.at[2]),
        pltpu.make_async_copy(v_ref.at[rows, head_cols(head_oth)], oth.at[:, pl.ds(HD, HD)], lsem.at[3]),
        pltpu.make_async_copy(q_ref, qall.at[co], lsem.at[4]),
    ]
    for copy in loads:
        copy.start()
    flag_load = pltpu.make_async_copy(flags_ref, flags, fsem)
    flag_load.start()
    w_own = pltpu.make_async_copy(
        w_ref.at[:, pl.ds(pl.multiple_of(co * COLS, COLS), COLS)], wv.at[co], wsem
    )
    w_own.start()

    barrier = pltpu.get_barrier_semaphore()
    peers = [zdev(way, d) for way in (0, 1) for d in (1, 2)] + [dev_a, dev_b_src, dev_c, mate, ydev(0), ydev(1)]
    peers += [xdev(d, cc) for d in (1, 2, 3) for cc in (0, 1)]
    for peer in peers:
        pl.semaphore_signal(barrier, inc=1, device_id=peer, device_id_type=MESH)
    pl.semaphore_wait(barrier, len(peers))

    def remote(src, dst, send_sem, recv_sem, peer):
        return pltpu.make_async_remote_copy(
            src_ref=src, dst_ref=dst, send_sem=send_sem, recv_sem=recv_sem, device_id=peer, device_id_type=MESH
        )

    def hop(way, d, step, j):
        zi = ahead(1 - way, d)
        at = d + step - 1
        return remote(kv.at[zi, j], kv.at[zi, j], tx.at[way, at, j], rx.at[way, at, j], zdev(way, step))

    def arrival(way, d, j):
        zi = ahead(1 - way, d)
        return remote(kv.at[zi, j], kv.at[zi, j], tx.at[way, d - 1, j], rx.at[way, d - 1, j], zdev(way, 1))

    def comes(zz, way, d, j):
        if j:
            return row_of[j] < r
        return ((way == 0) & (zz >= d)) | ((way == 1) & ((zz + d >= NZ) | (zz + d <= 4)))

    def farthest(way, j):
        return 6 - way if j < 2 else 5 + way

    def goes(way, d, step, j):
        return (d + step <= farthest(way, j)) & comes(ahead(way, step), way, d + step, j)

    def send_on(way, d, j):
        for step in (2, 1):

            @pl.when(goes(way, d, step, j))
            def _():
                hop(way, d, step, j).start()

    def clear(zi, carry):
        @pl.when((zi > z) & (zi > 4))
        def _():
            kv[zi, 0] = jnp.zeros((HALF, 2 * HD), BF16)

        for j in (1, 2, 3):

            @pl.when(row_of[j] > r)
            def _():
                kv[zi, j] = jnp.zeros((HALF, 2 * HD), BF16)

        return carry

    for copy in loads[:2]:
        copy.wait()
    for way in (0, 1):
        send_on(way, 0, 0)
    for copy in loads[2:4]:
        copy.wait()
    y_copies = [
        remote(oth, kv.at[z, 1], ytx.at[0], yrx.at[0], dev_a),
        remote(kv.at[z, 0], kv.at[z, 2], ytx.at[1], yrx.at[1], dev_b),
        remote(oth, kv.at[z, 3], ytx.at[2], yrx.at[2], dev_c),
    ]
    y_rows = (r_minus, r_minus, r_far)
    for i in (2, 1, 0):

        @pl.when(y_rows[i] > r)
        def _():
            y_copies[i].start()

    q_copy = remote(q_ref, qall.at[co], qsem.at[0], qsem.at[1], mate)
    q_copy.start()
    w_copy = remote(
        w_ref.at[:, pl.ds(pl.multiple_of((1 - co) * COLS, COLS), COLS)], wv.at[co], wrem.at[0], wrem.at[1], mate
    )
    w_copy.start()

    lane = lax.broadcasted_iota(jnp.int32, (1, 2 * TOK), 1)
    first_half = lax.rem(lane, TOK) < HALF

    loads[4].wait()
    q_copy.wait_recv()
    for i in range(8):
        side = slice((i % 2) * TOK, (i % 2 + 1) * TOK)
        qt[i // 2, :, side] = qall[i // 4, :, (i % 4) * HD : (i % 4 + 1) * HD].T
    for g in range(4):
        acc[g, :HD] = jnp.zeros((HD, 2 * TOK), F32)
        acc[g, HD : HD + 8] = jnp.where(
            lax.broadcasted_iota(jnp.int32, (8, 2 * TOK), 0) == 0, FLOOR, 0.0
        )

    for j in (1, 2, 3):

        @pl.when(row_of[j] < r)
        def _():
            y_copies[j - 1].wait_recv()

        for way in (0, 1):
            send_on(way, 0, j)

    lax.fori_loop(0, NZ, clear, 0)
    flag_load.wait()
    def prepare(slot, zi):
        vt[slot] = kv[zi, :, :, HD:].reshape(4 * HALF, HD).T

    def attend(bundles, g, diagonal=False):
        query = qt[g]
        old = acc[g, HD : HD + 1]
        new = old
        tiles = []
        for slot, zi in bundles:
            keys = kv[zi, :, :, :HD].reshape(4 * HALF, HD)
            scores = jnp.dot(keys, query, preferred_element_type=F32)
            parts = []
            for j in range(4):
                at = 2 * (row_of[j] * NZ + zi) + co
                flag = jnp.where(first_half, flags[0, at], flags[1, at]).astype(F32)
                bias = (flag - 1.0) * NEG
                if diagonal and j == 0:
                    key_pos = co * HALF + lax.broadcasted_iota(jnp.int32, (HALF, 2 * TOK), 0)
                    query_pos = lax.rem(lax.broadcasted_iota(jnp.int32, (HALF, 2 * TOK), 1), TOK)
                    bias = jnp.where(key_pos <= query_pos, bias, -NEG)
                parts.append(scores[j * HALF : (j + 1) * HALF] * SCALE + bias)
            scores = jnp.concatenate(parts, axis=0)
            new = jnp.maximum(new, jnp.max(scores, axis=0, keepdims=True))
            tiles.append(scores)
        factor = jnp.exp2(old - new)
        total = acc[g, HD + 1 : HD + 2] * factor
        mixed = acc[g, :HD] * factor
        for (slot, _), scores in zip(bundles, tiles):
            weights = jnp.exp2(scores - new)
            total = total + jnp.sum(weights, axis=0, keepdims=True)
            mixed = mixed + jnp.dot(vt[slot], weights.astype(BF16), preferred_element_type=F32)
        acc[g, HD : HD + 1] = new
        acc[g, HD + 1 : HD + 2] = total
        acc[g, :HD] = mixed

    def relay(way, d, j):
        @pl.when((d <= farthest(way, j)) & comes(z, way, d, j))
        def _():
            arrival(way, d, j).wait_recv()

        @pl.when(lax.rem(d, 2) == 0)
        def _():
            send_on(way, d, j)

    def packed(*steps):
        return sum((8 * way + d) * 16**i for i, (way, d) in enumerate(steps))

    def by_place(first, second, other):
        return jnp.where(z == 0, first, jnp.where(z == 1, second, other))

    order_a = by_place(
        packed((1, 2), (1, 4), (0, 2), (0, 4), (0, 5), (0, 6)),
        packed((1, 2), (0, 1), (1, 4), (0, 4), (0, 5), (0, 6)),
        packed((0, 2), (0, 1), (0, 4), (0, 3), (0, 5), (0, 6)),
    )
    order_b = by_place(
        packed((1, 1), (1, 3), (0, 1), (1, 5), (0, 3), (1, 6)),
        packed((1, 1), (1, 3), (0, 2), (0, 3), (1, 5), (1, 6)),
        packed((1, 2), (1, 1), (1, 4), (1, 3), (1, 5), (1, 6)),
    )

    def unpack(code):
        digit = lax.rem(code, 16)
        return lax.div(digit, 8), lax.rem(digit, 8)

    pair = (unpack(order_a), unpack(order_b))
    for j in range(4):
        for way, d in pair:
            relay(way, d, j)
        if j == 0:
            prepare(0, z)
        attend([(0, z)], j, diagonal=True)

    def step(i, carry):
        code_a, code_b, held_a, held_b = carry
        pair = (unpack(code_a), unpack(code_b))
        for j in range(4):
            for way, d in pair:
                relay(way, d, j)
            if j == 0:
                prepare(0, held_a)
                prepare(1, held_b)
            attend([(0, held_a), (1, held_b)], j)
        held = [ahead(1 - way, d) for way, d in pair]
        return lax.div(code_a, 16), lax.div(code_b, 16), held[0], held[1]

    held = [ahead(1 - way, d) for way, d in pair]
    lax.fori_loop(1, 6, step, (lax.div(order_a, 16), lax.div(order_b, 16), held[0], held[1]))

    a_copies = [remote(acc.at[g], racc.at[g], atx.at[g], arx.at[g], mate) for g in range(4)]
    prepare(0, ahead(0, 6))
    for g in range(4):
        attend([(0, ahead(0, 6))], g)
        a_copies[g].start()

    def place(xx, yy):
        dx = lax.rem(xx - x + NX + 3, NX)
        near = lax.rem(yy + yl, 2)
        by_y = dx + 4 * (1 - near)
        by_x = dx * 2 + near
        return jnp.where(co == 0, by_y, by_x)

    for g in range(4):
        a_copies[g].wait_recv()
        m0, m1 = acc[g, HD : HD + 1], racc[g, HD : HD + 1]
        top = jnp.maximum(m0, m1)
        e0, e1 = jnp.exp2(m0 - top), jnp.exp2(m1 - top)
        total = acc[g, HD + 1 : HD + 2] * e0 + racc[g, HD + 1 : HD + 2] * e1
        mixed = (acc[g, :HD] * e0 + racc[g, :HD] * e1) / total
        for i in (0, 1):
            tile = mixed[:, i * TOK : (i + 1) * TOK].T.astype(BF16)
            cols = slice((2 * g + i) * HD, (2 * g + i + 1) * HD)
            for xx in range(4):
                for yy in range(2):
                    at = (xx * 2 + yy) * 16
                    a2[place(xx, yy), :, cols] = tile[at : at + 16]

    w_own.wait()
    w_copy.wait_recv()

    def send1y(n):
        return remote(sbuf.at[n, pl.ds(0, 64)], r1.at[n], t1.at[0, n], q1.at[0, n], ydev(0))

    def send1x(n, d):
        return remote(
            sbuf.at[n, pl.ds(32 * (d - 1), 32)], r1x.at[d - 1, n], t1.at[d - 1, n], q1.at[d - 1, n], xdev(d, 1)
        )

    def project(n, carry):
        cols = pl.ds(pl.multiple_of(n * CW, CW), CW)
        part = jnp.dot(
            a2[...].reshape(TOK, 8 * HD), wv[:, :, cols].reshape(8 * HD, CW), preferred_element_type=F32
        )
        sbuf[n] = part[:96].astype(BF16)
        own[n] = part[64:]

        @pl.when(co == 0)
        def _():
            send1y(n).start()

        @pl.when(co == 1)
        def _():
            for d in (2, 1, 3):
                send1x(n, d).start()

        return carry

    lax.fori_loop(0, NC, project, 0)

    def send2x(n, d, cc):
        return remote(s2a.at[n, d - 1, cc], f0.at[d - 1, n], t2.at[d - 1, cc, n], q2.at[d - 1, n], xdev(d, cc))

    def send2y(n, cc):
        return remote(s2b.at[n, cc], f1.at[0, n], t2.at[0, cc, n], q2.at[3, n], ydev(cc))

    def put(side, n):
        at = pl.multiple_of(side * COLS + n * CW, CW)
        return pltpu.make_async_copy(obuf.at[side, n], out_ref.at[:, pl.ds(at, CW)], osem.at[side, n])

    def send3a(n):
        return remote(s2d.at[n], f0.at[3, n], t3.at[n], q3.at[n], mate)

    def send3b(n):
        return remote(s2d.at[n], f1.at[1, n], t3.at[n], q3.at[n], mate)

    @pl.when(co == 0)
    def _():
        def second(n, carry):
            send1y(n).wait_recv()
            total = own[n] + r1[n].astype(F32)
            for d in (2, 1, 3):
                for cc in (0, 1):
                    at = 16 * (d - 1) + 8 * cc
                    s2a[n, d - 1, cc] = total[at : at + 8].astype(BF16)
                    send2x(n, d, cc).start()
            own2[n] = total[48:56]
            s2d[n] = total[56:].astype(BF16)
            send3a(n).start()
            return carry

        lax.fori_loop(0, NC, second, 0)

        def last(n, carry):
            for d in (1, 2, 3):
                send2x(n, d, 0).wait_recv()
            total = own2[n] + f0[0, n].astype(F32) + f0[1, n].astype(F32) + f0[2, n].astype(F32)
            obuf[0, n] = total.astype(BF16)
            put(0, n).start()
            send2y(n, 0).wait_recv()
            send3b(n).wait_recv()
            total = f1[0, n].astype(F32) + f1[1, n].astype(F32)
            obuf[1, n] = total.astype(BF16)
            put(1, n).start()
            return carry

        lax.fori_loop(0, NC, last, 0)

        def sent(n, carry):
            send1y(n).wait_send()
            for d in (1, 2, 3):
                for cc in (0, 1):
                    send2x(n, d, cc).wait_send()
            send3a(n).wait_send()
            return carry

        lax.fori_loop(0, NC, sent, 0)

    @pl.when(co == 1)
    def _():
        def second(n, carry):
            for d in (1, 2, 3):
                send1x(n, d).wait_recv()
            total = own[n, pl.ds(32, 32)]
            for d in range(3):
                total = total + r1x[d, n].astype(F32)
            for cc in (0, 1):
                s2b[n, cc] = total[16 + 8 * cc : 24 + 8 * cc].astype(BF16)
                send2y(n, cc).start()
            s2d[n] = total[:8].astype(BF16)
            send3b(n).start()
            own2[n] = total[8:16]
            return carry

        lax.fori_loop(0, NC, second, 0)

        def last(n, carry):
            for d in (1, 2, 3):
                send2x(n, d, 1).wait_recv()
            send3a(n).wait_recv()
            total = f0[3, n].astype(F32) + f0[0, n].astype(F32) + f0[1, n].astype(F32) + f0[2, n].astype(F32)
            obuf[0, n] = total.astype(BF16)
            put(0, n).start()
            send2y(n, 1).wait_recv()
            total = own2[n] + f1[0, n].astype(F32)
            obuf[1, n] = total.astype(BF16)
            put(1, n).start()
            return carry

        lax.fori_loop(0, NC, last, 0)

        def sent(n, carry):
            for d in (1, 2, 3):
                send1x(n, d).wait_send()
            for cc in (0, 1):
                send2y(n, cc).wait_send()
            send3b(n).wait_send()
            return carry

        lax.fori_loop(0, NC, sent, 0)

    def stored(n, carry):
        for side in (0, 1):
            put(side, n).wait()
        return carry

    lax.fori_loop(0, NC, stored, 0)

    for copy in [q_copy, w_copy] + a_copies:
        copy.wait_send()
    for i in range(3):

        @pl.when(y_rows[i] > r)
        def _():
            y_copies[i].wait_send()

    def drain(i, carry):
        d = 2 * i
        for j in range(4):
            for way in (0, 1):
                for step in (2, 1):

                    @pl.when(goes(way, d, step, j))
                    def _():
                        hop(way, d, step, j).wait_send()

        return carry

    lax.fori_loop(0, 3, drain, 0)


def local(queries, key_rows, value_rows, block_flags, out_weight):
    dma = pltpu.SemaphoreType.DMA
    hbm = pl.BlockSpec(memory_space=pl.ANY)
    vmem = pltpu.VMEM
    return pl.pallas_call(
        kernel,
        out_shape=jax.ShapeDtypeStruct((8, 2 * COLS), BF16),
        in_specs=[hbm] * 5,
        out_specs=hbm,
        scratch_shapes=[
            pltpu.SMEM((2, 96), jnp.int32),
            vmem((2, NC, 8, CW), BF16),
            vmem((NZ, 4, HALF, 2 * HD), BF16),
            vmem((HALF, 2 * HD), BF16),
            vmem((2, TOK, 4 * HD), BF16),
            vmem((4, HD, 2 * TOK), BF16),
            vmem((2, HD, 4 * HALF), BF16),
            vmem((4, HD + 8, 2 * TOK), F32),
            vmem((4, HD + 8, 2 * TOK), F32),
            vmem((8, 16, 8 * HD), BF16),
            vmem((2, 4 * HD, COLS), BF16),
            vmem((NC, 96, CW), BF16),
            vmem((NC, 64, CW), F32),
            vmem((NC, 64, CW), BF16),
            vmem((3, NC, 32, CW), BF16),
            vmem((NC, 3, 2, 8, CW), BF16),
            vmem((NC, 2, 8, CW), BF16),
            vmem((NC, 8, CW), BF16),
            vmem((4, NC, 8, CW), BF16),
            vmem((2, NC, 8, CW), BF16),
            vmem((NC, 8, CW), F32),
            dma((5,)),
            dma,
            dma,
            dma((2, NC)),
            dma((3,)),
            dma((3,)),
            dma((2, 6, 4)),
            dma((2, 6, 4)),
            dma((2,)),
            dma((2,)),
            dma((4,)),
            dma((4,)),
            dma((3, NC)),
            dma((3, NC)),
            dma((3, 2, NC)),
            dma((4, NC)),
            dma((NC,)),
            dma((NC,)),
        ],
        compiler_params=pltpu.CompilerParams(
            collective_id=0, has_side_effects=True, vmem_limit_bytes=60 * 2**20
        ),
        name="attention_layer",
    )(queries, key_rows, value_rows, block_flags, out_weight)


def solution(mesh):
    placed = (P("ctx", "head"), P("ctx", None), P("ctx", None), P("ctx", None), P("head", None))
    return jax.shard_map(
        local, mesh=mesh, in_specs=placed, out_specs=P(("ctx", "head"), None), check_vma=False
    )
```

```python
import math

import jax
import jax.numpy as jnp
from jax import lax
from jax.experimental import pallas as pl
from jax.experimental.pallas import tpu as pltpu
from jax.sharding import PartitionSpec as P

MESH = pl.DeviceIdType.MESH
HD = 128
TOK = 128
HALF = 64
NZ = 12
NX = 4
NR = 4
COLS = 4096
CW = 512
NC = COLS // CW
SCALE = math.log2(math.e) / math.sqrt(HD)
NEG = 1e30
FLOOR = -1e20
F32 = jnp.float32
BF16 = jnp.bfloat16


def kernel(
    q_ref, k_ref, v_ref, flags_ref, w_ref, out_ref,
    flags, obuf, kv, oth, qall, qt, vt, acc, racc, a2, wv, sbuf, own, r1, r1x, s2a, s2b, s2d, f0, f1, own2,
    lsem, wsem, fsem, osem, ytx, yrx, tx, rx, utx, urx, qsem, wrem, atx, arx, t1, q1, t2, q2, t3, q3,
):
    c = lax.axis_index("ctx")
    h = lax.axis_index("head")
    r, z = lax.div(c, NZ), lax.rem(c, NZ)
    x, yl, co = lax.div(h, 4), lax.rem(lax.div(h, 2), 2), lax.rem(h, 2)
    sg = 1 - 2 * yl

    def dev(rr, zz, xx, yy, cc):
        return {"ctx": rr * NZ + zz, "head": xx * 4 + yy * 2 + cc}

    def ahead(way, d):
        return lax.rem(z + NZ + (1 - 2 * way) * d, NZ)

    def zdev(way, d):
        return dev(r, ahead(way, d), x, yl, co)

    r_minus, r_plus, r_far = lax.rem(r - sg + NR, NR), lax.rem(r + sg + NR, NR), lax.rem(r + 2, NR)
    dev_a = dev(r_minus, z, x, 1 - yl, co)
    dev_b = dev(r_minus, z, x, yl, co)
    dev_c = dev(r_far, z, x, 1 - yl, co)
    mate = dev(r, z, x, yl, 1 - co)

    def xdev(d, cc):
        return dev(r, z, lax.rem(x + d, NX), yl, cc)

    def ydev(cc):
        return dev(r, z, x, 1 - yl, cc)

    row_of = (r, r_minus, r_plus, r_far)

    head_own = x * 2 + yl
    head_oth = x * 2 + 1 - yl
    rows = pl.ds(pl.multiple_of(co * HALF, HALF), HALF)

    def head_cols(kvh):
        return pl.ds(pl.multiple_of(kvh * HD, HD), HD)

    loads = [
        pltpu.make_async_copy(k_ref.at[rows, head_cols(head_own)], kv.at[z, 0, :, pl.ds(0, HD)], lsem.at[0]),
        pltpu.make_async_copy(v_ref.at[rows, head_cols(head_own)], kv.at[z, 0, :, pl.ds(HD, HD)], lsem.at[1]),
        pltpu.make_async_copy(k_ref.at[rows, head_cols(head_oth)], oth.at[:, pl.ds(0, HD)], lsem.at[2]),
        pltpu.make_async_copy(v_ref.at[rows, head_cols(head_oth)], oth.at[:, pl.ds(HD, HD)], lsem.at[3]),
        pltpu.make_async_copy(q_ref, qall.at[co], lsem.at[4]),
    ]
    for copy in loads:
        copy.start()
    flag_load = pltpu.make_async_copy(flags_ref, flags, fsem)
    flag_load.start()
    w_own = pltpu.make_async_copy(
        w_ref.at[:, pl.ds(pl.multiple_of(co * COLS, COLS), COLS)], wv.at[co], wsem
    )
    w_own.start()

    barrier = pltpu.get_barrier_semaphore()
    peers = [zdev(way, d) for way in (0, 1) for d in (1, 2)] + [dev_a, dev_c, mate, ydev(0), ydev(1)]
    peers += [dev(rr, z, x, yl, co) for rr in (r_plus, r_minus, r_far)]
    peers += [xdev(d, cc) for d in (1, 2, 3) for cc in (0, 1)]
    for peer in peers:
        pl.semaphore_signal(barrier, inc=1, device_id=peer, device_id_type=MESH)
    pl.semaphore_wait(barrier, len(peers))

    def remote(src, dst, send_sem, recv_sem, peer):
        return pltpu.make_async_remote_copy(
            src_ref=src, dst_ref=dst, send_sem=send_sem, recv_sem=recv_sem, device_id=peer, device_id_type=MESH
        )

    def hop(way, d, step, j):
        zi = ahead(1 - way, d)
        at = d + step - 1
        return remote(kv.at[zi, j], kv.at[zi, j], tx.at[way, at, j], rx.at[way, at, j], zdev(way, step))

    def arrival(way, d, j):
        zi = ahead(1 - way, d)
        return remote(kv.at[zi, j], kv.at[zi, j], tx.at[way, d - 1, j], rx.at[way, d - 1, j], zdev(way, 1))

    def comes(zz, way, d, j):
        if j:
            late = ((way == 0) & (zz < d)) | ((way == 1) & (zz <= 5) & (zz + d >= 6))
            return (row_of[j] < r) & jnp.logical_not(late)
        source = zz + d
        forth = (way == 0) & ((zz >= d) | (r < NR - 1))
        back = (way == 1) & ((source >= NZ) | (source <= 4) | ((source >= 6) & (r < NR - 1)))
        return forth | back

    def farthest(way, j):
        return 6 - way if j < 2 else 5 + way

    def goes(way, d, step, j):
        return (d + step <= farthest(way, j)) & comes(ahead(way, step), way, d + step, j)

    def send_on(way, d, j):
        for step in (2, 1):

            @pl.when(goes(way, d, step, j))
            def _():
                hop(way, d, step, j).start()

    def clear(zi, carry):
        @pl.when((zi > z) & ((zi == 5) | ((zi > 5) & (r == NR - 1))))
        def _():
            kv[zi, 0] = jnp.zeros((HALF, 2 * HD), BF16)

        for j in (1, 2, 3):

            @pl.when(row_of[j] > r)
            def _():
                kv[zi, j] = jnp.zeros((HALF, 2 * HD), BF16)

        return carry

    for copy in loads[:2]:
        copy.wait()
    for way in (0, 1):
        send_on(way, 0, 0)
    for copy in loads[2:4]:
        copy.wait()
    y_copies = [
        remote(oth, kv.at[z, 1], ytx.at[0], yrx.at[0], dev_a),
        remote(kv.at[z, 0], kv.at[z, 2], ytx.at[1], yrx.at[1], dev_b),
        remote(oth, kv.at[z, 3], ytx.at[2], yrx.at[2], dev_c),
    ]
    y_rows = (r_minus, r_minus, r_far)
    for i in (2, 1, 0):

        @pl.when(y_rows[i] > r)
        def _():
            y_copies[i].start()

    q_copy = remote(q_ref, qall.at[co], qsem.at[0], qsem.at[1], mate)
    q_copy.start()
    w_copy = remote(
        w_ref.at[:, pl.ds(pl.multiple_of((1 - co) * COLS, COLS), COLS)], wv.at[co], wrem.at[0], wrem.at[1], mate
    )
    w_copy.start()

    lane = lax.broadcasted_iota(jnp.int32, (1, 2 * TOK), 1)
    first_half = lax.rem(lane, TOK) < HALF

    loads[4].wait()
    q_copy.wait_recv()
    for i in range(8):
        side = slice((i % 2) * TOK, (i % 2 + 1) * TOK)
        qt[i // 2, :, side] = qall[i // 4, :, (i % 4) * HD : (i % 4 + 1) * HD].T
    for g in range(4):
        acc[g, :HD] = jnp.zeros((HD, 2 * TOK), F32)
        acc[g, HD : HD + 8] = jnp.where(
            lax.broadcasted_iota(jnp.int32, (8, 2 * TOK), 0) == 0, FLOOR, 0.0
        )

    for j in (1, 2, 3):

        @pl.when(row_of[j] < r)
        def _():
            y_copies[j - 1].wait_recv()

        for way in (0, 1):
            send_on(way, 0, j)

    lax.fori_loop(0, NZ, clear, 0)
    flag_load.wait()
    def prepare(slot, zi):
        vt[slot] = kv[zi, :, :, HD:].reshape(4 * HALF, HD).T

    def attend(bundles, g, diagonal=False):
        query = qt[g]
        old = acc[g, HD : HD + 1]
        new = old
        tiles = []
        for slot, zi in bundles:
            keys = kv[zi, :, :, :HD].reshape(4 * HALF, HD)
            scores = jnp.dot(keys, query, preferred_element_type=F32)
            parts = []
            for j in range(4):
                at = 2 * (row_of[j] * NZ + zi) + co
                flag = jnp.where(first_half, flags[0, at], flags[1, at]).astype(F32)
                bias = (flag - 1.0) * NEG
                if diagonal and j == 0:
                    key_pos = co * HALF + lax.broadcasted_iota(jnp.int32, (HALF, 2 * TOK), 0)
                    query_pos = lax.rem(lax.broadcasted_iota(jnp.int32, (HALF, 2 * TOK), 1), TOK)
                    bias = jnp.where(key_pos <= query_pos, bias, -NEG)
                parts.append(scores[j * HALF : (j + 1) * HALF] * SCALE + bias)
            scores = jnp.concatenate(parts, axis=0)
            new = jnp.maximum(new, jnp.max(scores, axis=0, keepdims=True))
            tiles.append(scores)
        factor = jnp.exp2(old - new)
        total = acc[g, HD + 1 : HD + 2] * factor
        mixed = acc[g, :HD] * factor
        for (slot, _), scores in zip(bundles, tiles):
            weights = jnp.exp2(scores - new)
            total = total + jnp.sum(weights, axis=0, keepdims=True)
            mixed = mixed + jnp.dot(vt[slot], weights.astype(BF16), preferred_element_type=F32)
        acc[g, HD : HD + 1] = new
        acc[g, HD + 1 : HD + 2] = total
        acc[g, :HD] = mixed

    def lift(zi, j):
        rr = (r, r_plus, r_minus, r_far)[j]
        return remote(kv.at[zi, 0], kv.at[zi, j], utx.at[zi - 6, j], urx.at[zi - 6, j], dev(rr, z, x, yl, co))

    def lifted(zi, j):
        return remote(kv.at[zi, j], kv.at[zi, j], utx.at[zi - 6, j], urx.at[zi - 6, j], dev(r_plus, z, x, yl, co))

    def relay(way, d, j):
        zi = ahead(1 - way, d)
        here = (d <= farthest(way, j)) & comes(z, way, d, j)
        late = (zi > 5) & (z <= 5) & (d <= farthest(way, j))

        @pl.when(here)
        def _():
            arrival(way, d, j).wait_recv()

        @pl.when(lax.rem(d, 2) == 0)
        def _():
            send_on(way, d, j)

        if j == 0:
            for i in (1, 2, 3):

                @pl.when(here & late & ((r, r_plus, r_minus, r_far)[i] > r))
                def _():
                    lift(zi, i).start()
        else:

            @pl.when(late & (row_of[j] < r))
            def _():
                lifted(zi, j).wait_recv()

    def packed(*steps):
        return sum((8 * way + d) * 16**i for i, (way, d) in enumerate(steps))

    def by_place(first, second, other):
        return jnp.where(z == 0, first, jnp.where(z == 1, second, other))

    order_a = by_place(
        packed((1, 2), (1, 4), (0, 2), (0, 4), (0, 5), (0, 6)),
        packed((1, 2), (0, 1), (1, 4), (0, 4), (0, 5), (0, 6)),
        packed((0, 2), (0, 1), (0, 4), (0, 3), (0, 5), (0, 6)),
    )
    order_b = by_place(
        packed((1, 1), (1, 3), (0, 1), (1, 5), (0, 3), (1, 6)),
        packed((1, 1), (1, 3), (0, 2), (0, 3), (1, 5), (1, 6)),
        packed((1, 2), (1, 1), (1, 4), (1, 3), (1, 5), (1, 6)),
    )

    def unpack(code):
        digit = lax.rem(code, 16)
        return lax.div(digit, 8), lax.rem(digit, 8)

    pair = (unpack(order_a), unpack(order_b))
    order_a, order_b = lax.div(order_a, 16), lax.div(order_b, 16)
    after = (unpack(order_a), unpack(order_b))
    for way, d in pair:
        relay(way, d, 0)
    for j in range(4):
        for way, d in pair if j else after:
            relay(way, d, j)
        if j == 0:
            prepare(0, z)
        attend([(0, z)], j, diagonal=True)

    def step(i, carry):
        code_a, code_b, held_a, held_b = carry
        pair = (unpack(code_a), unpack(code_b))
        code_a, code_b = lax.div(code_a, 16), lax.div(code_b, 16)
        after = (unpack(code_a), unpack(code_b))
        for j in range(4):
            if j == 0:

                @pl.when(i < 5)
                def _():
                    for way, d in after:
                        relay(way, d, 0)

                prepare(0, held_a)
                prepare(1, held_b)
            else:
                for way, d in pair:
                    relay(way, d, j)
            attend([(0, held_a), (1, held_b)], j)
        held = [ahead(1 - way, d) for way, d in pair]
        return code_a, code_b, held[0], held[1]

    held = [ahead(1 - way, d) for way, d in pair]
    lax.fori_loop(1, 6, step, (order_a, order_b, held[0], held[1]))

    a_copies = [remote(acc.at[g], racc.at[g], atx.at[g], arx.at[g], mate) for g in range(4)]
    prepare(0, ahead(0, 6))
    for g in range(4):
        attend([(0, ahead(0, 6))], g)
        a_copies[g].start()

    def place(xx, yy):
        dx = lax.rem(xx - x + NX + 3, NX)
        near = lax.rem(yy + yl, 2)
        by_y = dx + 4 * (1 - near)
        by_x = dx * 2 + near
        return jnp.where(co == 0, by_y, by_x)

    for g in range(4):
        a_copies[g].wait_recv()
        m0, m1 = acc[g, HD : HD + 1], racc[g, HD : HD + 1]
        top = jnp.maximum(m0, m1)
        e0, e1 = jnp.exp2(m0 - top), jnp.exp2(m1 - top)
        total = acc[g, HD + 1 : HD + 2] * e0 + racc[g, HD + 1 : HD + 2] * e1
        mixed = (acc[g, :HD] * e0 + racc[g, :HD] * e1) / total
        for i in (0, 1):
            tile = mixed[:, i * TOK : (i + 1) * TOK].T.astype(BF16)
            cols = slice((2 * g + i) * HD, (2 * g + i + 1) * HD)
            for xx in range(4):
                for yy in range(2):
                    at = (xx * 2 + yy) * 16
                    a2[place(xx, yy), :, cols] = tile[at : at + 16]

    w_own.wait()
    w_copy.wait_recv()

    def send1y(n):
        return remote(sbuf.at[n, pl.ds(0, 64)], r1.at[n], t1.at[0, n], q1.at[0, n], ydev(0))

    def send1x(n, d):
        return remote(
            sbuf.at[n, pl.ds(32 * (d - 1), 32)], r1x.at[d - 1, n], t1.at[d - 1, n], q1.at[d - 1, n], xdev(d, 1)
        )

    def project(n, carry):
        cols = pl.ds(pl.multiple_of(n * CW, CW), CW)
        part = jnp.dot(
            a2[...].reshape(TOK, 8 * HD), wv[:, :, cols].reshape(8 * HD, CW), preferred_element_type=F32
        )
        sbuf[n] = part[:96].astype(BF16)
        own[n] = part[64:]

        @pl.when(co == 0)
        def _():
            send1y(n).start()

        @pl.when(co == 1)
        def _():
            for d in (2, 1, 3):
                send1x(n, d).start()

        return carry

    lax.fori_loop(0, NC, project, 0)

    def send2x(n, d, cc):
        return remote(s2a.at[n, d - 1, cc], f0.at[d - 1, n], t2.at[d - 1, cc, n], q2.at[d - 1, n], xdev(d, cc))

    def send2y(n, cc):
        return remote(s2b.at[n, cc], f1.at[0, n], t2.at[0, cc, n], q2.at[3, n], ydev(cc))

    def put(side, n):
        at = pl.multiple_of(side * COLS + n * CW, CW)
        return pltpu.make_async_copy(obuf.at[side, n], out_ref.at[:, pl.ds(at, CW)], osem.at[side, n])

    def send3a(n):
        return remote(s2d.at[n], f0.at[3, n], t3.at[n], q3.at[n], mate)

    def send3b(n):
        return remote(s2d.at[n], f1.at[1, n], t3.at[n], q3.at[n], mate)

    @pl.when(co == 0)
    def _():
        def second(n, carry):
            send1y(n).wait_recv()
            total = own[n] + r1[n].astype(F32)
            for d in (2, 1, 3):
                for cc in (0, 1):
                    at = 16 * (d - 1) + 8 * cc
                    s2a[n, d - 1, cc] = total[at : at + 8].astype(BF16)
                    send2x(n, d, cc).start()
            own2[n] = total[48:56]
            s2d[n] = total[56:].astype(BF16)
            send3a(n).start()
            return carry

        lax.fori_loop(0, NC, second, 0)

        def last(n, carry):
            for d in (1, 2, 3):
                send2x(n, d, 0).wait_recv()
            total = own2[n] + f0[0, n].astype(F32) + f0[1, n].astype(F32) + f0[2, n].astype(F32)
            obuf[0, n] = total.astype(BF16)
            put(0, n).start()
            send2y(n, 0).wait_recv()
            send3b(n).wait_recv()
            total = f1[0, n].astype(F32) + f1[1, n].astype(F32)
            obuf[1, n] = total.astype(BF16)
            put(1, n).start()
            return carry

        lax.fori_loop(0, NC, last, 0)

        def sent(n, carry):
            send1y(n).wait_send()
            for d in (1, 2, 3):
                for cc in (0, 1):
                    send2x(n, d, cc).wait_send()
            send3a(n).wait_send()
            return carry

        lax.fori_loop(0, NC, sent, 0)

    @pl.when(co == 1)
    def _():
        def second(n, carry):
            for d in (1, 2, 3):
                send1x(n, d).wait_recv()
            total = own[n, pl.ds(32, 32)]
            for d in range(3):
                total = total + r1x[d, n].astype(F32)
            for cc in (0, 1):
                s2b[n, cc] = total[16 + 8 * cc : 24 + 8 * cc].astype(BF16)
                send2y(n, cc).start()
            s2d[n] = total[:8].astype(BF16)
            send3b(n).start()
            own2[n] = total[8:16]
            return carry

        lax.fori_loop(0, NC, second, 0)

        def last(n, carry):
            for d in (1, 2, 3):
                send2x(n, d, 1).wait_recv()
            send3a(n).wait_recv()
            total = f0[3, n].astype(F32) + f0[0, n].astype(F32) + f0[1, n].astype(F32) + f0[2, n].astype(F32)
            obuf[0, n] = total.astype(BF16)
            put(0, n).start()
            send2y(n, 1).wait_recv()
            total = own2[n] + f1[0, n].astype(F32)
            obuf[1, n] = total.astype(BF16)
            put(1, n).start()
            return carry

        lax.fori_loop(0, NC, last, 0)

        def sent(n, carry):
            for d in (1, 2, 3):
                send1x(n, d).wait_send()
            for cc in (0, 1):
                send2y(n, cc).wait_send()
            send3b(n).wait_send()
            return carry

        lax.fori_loop(0, NC, sent, 0)

    def stored(n, carry):
        for side in (0, 1):
            put(side, n).wait()
        return carry

    lax.fori_loop(0, NC, stored, 0)

    for copy in [q_copy, w_copy] + a_copies:
        copy.wait_send()
    for i in range(3):

        @pl.when(y_rows[i] > r)
        def _():
            y_copies[i].wait_send()

    def drain(i, carry):
        d = 2 * i
        for j in range(4):
            for way in (0, 1):
                for step in (2, 1):

                    @pl.when(goes(way, d, step, j))
                    def _():
                        hop(way, d, step, j).wait_send()

        return carry

    lax.fori_loop(0, 3, drain, 0)

    def passed(zi, carry):
        for i in (1, 2, 3):

            @pl.when((z <= 5) & ((r, r_plus, r_minus, r_far)[i] > r))
            def _():
                lift(zi, i).wait_send()

        return carry

    lax.fori_loop(6, NZ, passed, 0)


def local(queries, key_rows, value_rows, block_flags, out_weight):
    dma = pltpu.SemaphoreType.DMA
    hbm = pl.BlockSpec(memory_space=pl.ANY)
    vmem = pltpu.VMEM
    return pl.pallas_call(
        kernel,
        out_shape=jax.ShapeDtypeStruct((8, 2 * COLS), BF16),
        in_specs=[hbm] * 5,
        out_specs=hbm,
        scratch_shapes=[
            pltpu.SMEM((2, 96), jnp.int32),
            vmem((2, NC, 8, CW), BF16),
            vmem((NZ, 4, HALF, 2 * HD), BF16),
            vmem((HALF, 2 * HD), BF16),
            vmem((2, TOK, 4 * HD), BF16),
            vmem((4, HD, 2 * TOK), BF16),
            vmem((2, HD, 4 * HALF), BF16),
            vmem((4, HD + 8, 2 * TOK), F32),
            vmem((4, HD + 8, 2 * TOK), F32),
            vmem((8, 16, 8 * HD), BF16),
            vmem((2, 4 * HD, COLS), BF16),
            vmem((NC, 96, CW), BF16),
            vmem((NC, 64, CW), F32),
            vmem((NC, 64, CW), BF16),
            vmem((3, NC, 32, CW), BF16),
            vmem((NC, 3, 2, 8, CW), BF16),
            vmem((NC, 2, 8, CW), BF16),
            vmem((NC, 8, CW), BF16),
            vmem((4, NC, 8, CW), BF16),
            vmem((2, NC, 8, CW), BF16),
            vmem((NC, 8, CW), F32),
            dma((5,)),
            dma,
            dma,
            dma((2, NC)),
            dma((3,)),
            dma((3,)),
            dma((2, 6, 4)),
            dma((2, 6, 4)),
            dma((6, 4)),
            dma((6, 4)),
            dma((2,)),
            dma((2,)),
            dma((4,)),
            dma((4,)),
            dma((3, NC)),
            dma((3, NC)),
            dma((3, 2, NC)),
            dma((4, NC)),
            dma((NC,)),
            dma((NC,)),
        ],
        compiler_params=pltpu.CompilerParams(
            collective_id=0, has_side_effects=True, vmem_limit_bytes=60 * 2**20
        ),
        name="attention_layer",
    )(queries, key_rows, value_rows, block_flags, out_weight)


def solution(mesh):
    placed = (P("ctx", "head"), P("ctx", None), P("ctx", None), P("ctx", None), P("head", None))
    return jax.shard_map(
        local, mesh=mesh, in_specs=placed, out_specs=P(("ctx", "head"), None), check_vma=False
    )
```

```python
import math

import jax
import jax.numpy as jnp
from jax import lax
from jax.experimental import pallas as pl
from jax.experimental.pallas import tpu as pltpu
from jax.sharding import PartitionSpec as P

MESH = pl.DeviceIdType.MESH
HD = 128
TOK = 128
HALF = 64
NZ = 12
NX = 4
NR = 4
COLS = 4096
CW = 512
NC = COLS // CW
SCALE = math.log2(math.e) / math.sqrt(HD)
NEG = 1e30
FLOOR = -1e20
F32 = jnp.float32
BF16 = jnp.bfloat16


def kernel(
    q_ref, k_ref, v_ref, flags_ref, w_ref, out_ref,
    flags, obuf, kv, oth, qall, qt, vt, acc, racc, a2, wv, sbuf, own, r1, r1x, s2a, s2b, s2d, f0, f1, fm, own2,
    lsem, wsem, fsem, osem, ytx, yrx, tx, rx, qsem, wrem, atx, arx, t1, q1, t2, q2, t3, q3,
):
    c = lax.axis_index("ctx")
    h = lax.axis_index("head")
    r, z = lax.div(c, NZ), lax.rem(c, NZ)
    x, yl, co = lax.div(h, 4), lax.rem(lax.div(h, 2), 2), lax.rem(h, 2)
    sg = 1 - 2 * yl

    def dev(rr, zz, xx, yy, cc):
        return {"ctx": rr * NZ + zz, "head": xx * 4 + yy * 2 + cc}

    def ahead(way, d):
        return lax.rem(z + NZ + (1 - 2 * way) * d, NZ)

    def zdev(way, d):
        return dev(r, ahead(way, d), x, yl, co)

    r_minus, r_plus, r_far = lax.rem(r - sg + NR, NR), lax.rem(r + sg + NR, NR), lax.rem(r + 2, NR)
    dev_a = dev(r_minus, z, x, 1 - yl, co)
    dev_b = dev(r_minus, z, x, yl, co)
    dev_b_src = dev(r_plus, z, x, yl, co)
    dev_c = dev(r_far, z, x, 1 - yl, co)
    mate = dev(r, z, x, yl, 1 - co)

    def xdev(d, cc):
        return dev(r, z, lax.rem(x + d, NX), yl, cc)

    def ydev(cc):
        return dev(r, z, x, 1 - yl, cc)

    row_of = (r, r_minus, r_plus, r_far)

    head_own = x * 2 + yl
    head_oth = x * 2 + 1 - yl
    rows = pl.ds(pl.multiple_of(co * HALF, HALF), HALF)

    def head_cols(kvh):
        return pl.ds(pl.multiple_of(kvh * HD, HD), HD)

    loads = [
        pltpu.make_async_copy(k_ref.at[rows, head_cols(head_own)], kv.at[z, 0, :, pl.ds(0, HD)], lsem.at[0]),
        pltpu.make_async_copy(v_ref.at[rows, head_cols(head_own)], kv.at[z, 0, :, pl.ds(HD, HD)], lsem.at[1]),
        pltpu.make_async_copy(k_ref.at[rows, head_cols(head_oth)], oth.at[:, pl.ds(0, HD)], lsem.at[2]),
        pltpu.make_async_copy(v_ref.at[rows, head_cols(head_oth)], oth.at[:, pl.ds(HD, HD)], lsem.at[3]),
        pltpu.make_async_copy(q_ref, qall.at[co], lsem.at[4]),
    ]
    for copy in loads:
        copy.start()
    flag_load = pltpu.make_async_copy(flags_ref, flags, fsem)
    flag_load.start()
    w_own = pltpu.make_async_copy(
        w_ref.at[:, pl.ds(pl.multiple_of(co * COLS, COLS), COLS)], wv.at[co], wsem
    )
    w_own.start()

    barrier = pltpu.get_barrier_semaphore()
    peers = [zdev(way, d) for way in (0, 1) for d in (1, 2)] + [dev_a, dev_b_src, dev_c, mate, ydev(0), ydev(1)]
    peers += [xdev(d, cc) for d in (1, 2, 3) for cc in (0, 1)]
    for peer in peers:
        pl.semaphore_signal(barrier, inc=1, device_id=peer, device_id_type=MESH)
    pl.semaphore_wait(barrier, len(peers))

    def remote(src, dst, send_sem, recv_sem, peer):
        return pltpu.make_async_remote_copy(
            src_ref=src, dst_ref=dst, send_sem=send_sem, recv_sem=recv_sem, device_id=peer, device_id_type=MESH
        )

    def hop(way, d, step, j):
        zi = ahead(1 - way, d)
        at = d + step - 1
        return remote(kv.at[zi, j], kv.at[zi, j], tx.at[way, at, j], rx.at[way, at, j], zdev(way, step))

    def arrival(way, d, j):
        zi = ahead(1 - way, d)
        return remote(kv.at[zi, j], kv.at[zi, j], tx.at[way, d - 1, j], rx.at[way, d - 1, j], zdev(way, 1))

    def comes(zz, way, d, j):
        if j:
            return row_of[j] < r
        return ((way == 0) & (zz >= d)) | ((way == 1) & ((zz + d >= NZ) | (zz + d <= 4)))

    def farthest(way, j):
        return 6 - way if j < 2 else 5 + way

    def goes(way, d, step, j):
        if j:
            return (step == 1) & (d + 1 <= farthest(way, j)) & comes(ahead(way, 1), way, d + 1, j)
        return (lax.rem(d, 2) == 0) & (d + step <= farthest(way, j)) & comes(ahead(way, step), way, d + step, j)

    def send_on(way, d, j):
        for step in (1,) if j else (2, 1):

            @pl.when(goes(way, d, step, j))
            def _():
                hop(way, d, step, j).start()

    def clear(zi, carry):
        @pl.when((zi > z) & (zi > 4))
        def _():
            kv[zi, 0] = jnp.zeros((HALF, 2 * HD), BF16)

        for j in (1, 2, 3):

            @pl.when(row_of[j] > r)
            def _():
                kv[zi, j] = jnp.zeros((HALF, 2 * HD), BF16)

        return carry

    for copy in loads[:2]:
        copy.wait()
    for way in (0, 1):
        send_on(way, 0, 0)
    for copy in loads[2:4]:
        copy.wait()
    y_copies = [
        remote(oth, kv.at[z, 1], ytx.at[0], yrx.at[0], dev_a),
        remote(kv.at[z, 0], kv.at[z, 2], ytx.at[1], yrx.at[1], dev_b),
        remote(oth, kv.at[z, 3], ytx.at[2], yrx.at[2], dev_c),
    ]
    y_rows = (r_minus, r_minus, r_far)
    for i in (2, 1, 0):

        @pl.when(y_rows[i] > r)
        def _():
            y_copies[i].start()

    q_copy = remote(q_ref, qall.at[co], qsem.at[0], qsem.at[1], mate)
    q_copy.start()
    w_copy = remote(
        w_ref.at[:, pl.ds(pl.multiple_of((1 - co) * COLS, COLS), COLS)], wv.at[co], wrem.at[0], wrem.at[1], mate
    )
    w_copy.start()

    lane = lax.broadcasted_iota(jnp.int32, (1, 2 * TOK), 1)
    first_half = lax.rem(lane, TOK) < HALF

    loads[4].wait()
    q_copy.wait_recv()
    for i in range(8):
        side = slice((i % 2) * TOK, (i % 2 + 1) * TOK)
        qt[i // 2, :, side] = qall[i // 4, :, (i % 4) * HD : (i % 4 + 1) * HD].T
    for g in range(4):
        acc[g, :HD] = jnp.zeros((HD, 2 * TOK), F32)
        acc[g, HD : HD + 8] = jnp.where(
            lax.broadcasted_iota(jnp.int32, (8, 2 * TOK), 0) == 0, FLOOR, 0.0
        )

    for j in (1, 2, 3):

        @pl.when(row_of[j] < r)
        def _():
            y_copies[j - 1].wait_recv()

        for way in (0, 1):
            send_on(way, 0, j)

    lax.fori_loop(0, NZ, clear, 0)
    flag_load.wait()
    def prepare(slot, zi):
        vt[slot] = kv[zi, :, :, HD:].reshape(4 * HALF, HD).T

    def attend(bundles, g, diagonal=False):
        query = qt[g]
        old = acc[g, HD : HD + 1]
        new = old
        tiles = []
        for slot, zi in bundles:
            keys = kv[zi, :, :, :HD].reshape(4 * HALF, HD)
            scores = jnp.dot(keys, query, preferred_element_type=F32)
            parts = []
            for j in range(4):
                at = 2 * (row_of[j] * NZ + zi) + co
                flag = jnp.where(first_half, flags[0, at], flags[1, at]).astype(F32)
                bias = (flag - 1.0) * NEG
                if diagonal and j == 0:
                    key_pos = co * HALF + lax.broadcasted_iota(jnp.int32, (HALF, 2 * TOK), 0)
                    query_pos = lax.rem(lax.broadcasted_iota(jnp.int32, (HALF, 2 * TOK), 1), TOK)
                    bias = jnp.where(key_pos <= query_pos, bias, -NEG)
                parts.append(scores[j * HALF : (j + 1) * HALF] * SCALE + bias)
            scores = jnp.concatenate(parts, axis=0)
            new = jnp.maximum(new, jnp.max(scores, axis=0, keepdims=True))
            tiles.append(scores)
        factor = jnp.exp2(old - new)
        total = acc[g, HD + 1 : HD + 2] * factor
        mixed = acc[g, :HD] * factor
        for (slot, _), scores in zip(bundles, tiles):
            weights = jnp.exp2(scores - new)
            total = total + jnp.sum(weights, axis=0, keepdims=True)
            mixed = mixed + jnp.dot(vt[slot], weights.astype(BF16), preferred_element_type=F32)
        acc[g, HD : HD + 1] = new
        acc[g, HD + 1 : HD + 2] = total
        acc[g, :HD] = mixed

    def relay(way, d, j):
        @pl.when((d <= farthest(way, j)) & comes(z, way, d, j))
        def _():
            arrival(way, d, j).wait_recv()

        send_on(way, d, j)

    def packed(*steps):
        return sum((8 * way + d) * 16**i for i, (way, d) in enumerate(steps))

    def by_place(first, second, other):
        return jnp.where(z == 0, first, jnp.where(z == 1, second, other))

    order_a = by_place(
        packed((1, 1), (1, 3), (0, 1), (0, 3), (0, 4), (0, 6)),
        packed((1, 1), (1, 2), (0, 2), (0, 3), (0, 5), (0, 6)),
        packed((0, 1), (0, 2), (0, 3), (0, 4), (0, 5), (0, 6)),
    )
    order_b = by_place(
        packed((1, 2), (1, 4), (0, 2), (1, 5), (0, 5), (1, 6)),
        packed((0, 1), (1, 3), (1, 4), (0, 4), (1, 5), (1, 6)),
        packed((1, 1), (1, 2), (1, 3), (1, 4), (1, 5), (1, 6)),
    )

    def unpack(code):
        digit = lax.rem(code, 16)
        return lax.div(digit, 8), lax.rem(digit, 8)

    pair = (unpack(order_a), unpack(order_b))
    for j in range(4):
        for way, d in pair:
            relay(way, d, j)
        if j == 0:
            prepare(0, z)
        attend([(0, z)], j, diagonal=True)

    def step(i, carry):
        code_a, code_b, held_a, held_b = carry
        pair = (unpack(code_a), unpack(code_b))
        for j in range(4):
            for way, d in pair:
                relay(way, d, j)
            if j == 0:
                prepare(0, held_a)
                prepare(1, held_b)
            attend([(0, held_a), (1, held_b)], j)
        held = [ahead(1 - way, d) for way, d in pair]
        return lax.div(code_a, 16), lax.div(code_b, 16), held[0], held[1]

    held = [ahead(1 - way, d) for way, d in pair]
    lax.fori_loop(1, 6, step, (lax.div(order_a, 16), lax.div(order_b, 16), held[0], held[1]))

    a_copies = [remote(acc.at[g], racc.at[g], atx.at[g], arx.at[g], mate) for g in range(4)]
    prepare(0, ahead(0, 6))
    for g in range(4):
        attend([(0, ahead(0, 6))], g)
        a_copies[g].start()

    def places(xx, yy):
        dx = lax.rem(xx - x + NX + 3, NX)
        near = lax.rem(yy + yl, 2)
        return dx + 4 * (1 - near), dx * 2 + near

    for g in range(4):
        a_copies[g].wait_recv()
        m0, m1 = acc[g, HD : HD + 1], racc[g, HD : HD + 1]
        top = jnp.maximum(m0, m1)
        e0, e1 = jnp.exp2(m0 - top), jnp.exp2(m1 - top)
        total = acc[g, HD + 1 : HD + 2] * e0 + racc[g, HD + 1 : HD + 2] * e1
        mixed = (acc[g, :HD] * e0 + racc[g, :HD] * e1) / total
        for i in (0, 1):
            tile = mixed[:, i * TOK : (i + 1) * TOK].T.astype(BF16)
            cols = slice((2 * g + i) * HD, (2 * g + i + 1) * HD)
            for xx in range(4):
                for yy in range(2):
                    at = (xx * 2 + yy) * 16
                    for kind, place in enumerate(places(xx, yy)):
                        a2[kind, place, :, cols] = tile[at : at + 16]

    w_own.wait()
    w_copy.wait_recv()

    def send1y(m):
        return remote(sbuf.at[2 * m, pl.ds(0, 64)], r1.at[m], t1.at[3, m], q1.at[3, m], ydev(co))

    def send1x(m, d):
        rows = pl.ds(32 * (d - 1), 32)
        return remote(sbuf.at[2 * m + 1, rows], r1x.at[d - 1, m], t1.at[d - 1, m], q1.at[d - 1, m], xdev(d, co))

    def project(m, carry):
        for kind in (1, 0):
            n = 2 * m + kind
            cols = pl.ds(pl.multiple_of(n * CW, CW), CW)
            part = jnp.dot(
                a2[kind].reshape(TOK, 8 * HD), wv[:, :, cols].reshape(8 * HD, CW), preferred_element_type=F32
            )
            sbuf[n] = part[:96].astype(BF16)
            own[n] = part[64:]
            if kind:
                for d in (2, 1, 3):
                    send1x(m, d).start()
            else:
                send1y(m).start()
        return carry

    lax.fori_loop(0, NC // 2, project, 0)

    def send2x(m, d, cc, side):
        return remote(s2a.at[m, d - 1, cc], f0.at[side, d - 1, m], t2.at[d - 1, cc, m], q2.at[side, d - 1, m], xdev(d, cc))

    def send2y(m, cc, side):
        return remote(s2b.at[m, cc], f1.at[side, m], t2.at[3, cc, m], q2.at[side, 3, m], ydev(cc))

    def send3(n):
        return remote(s2d.at[n, 1 - co], fm.at[n], t3.at[n], q3.at[n], mate)

    def keep(n, total):
        for cc in (0, 1):
            own2[n, cc] = total[8 * cc : 8 * cc + 8]
            s2d[n, cc] = total[8 * cc : 8 * cc + 8].astype(BF16)
        send3(n).start()

    def second(m, carry):
        for d in (1, 2, 3):
            send1x(m, d).wait_recv()
        total = own[2 * m + 1, pl.ds(32, 32)]
        for d in range(3):
            total = total + r1x[d, m].astype(F32)
        for cc in (0, 1):
            s2b[m, cc] = total[16 + 8 * cc : 24 + 8 * cc].astype(BF16)
            send2y(m, cc, co).start()
        keep(2 * m + 1, total[:16])
        send1y(m).wait_recv()
        total = own[2 * m] + r1[m].astype(F32)
        for d in (2, 1, 3):
            for cc in (0, 1):
                at = 16 * (d - 1) + 8 * cc
                s2a[m, d - 1, cc] = total[at : at + 8].astype(BF16)
                send2x(m, d, cc, co).start()
        keep(2 * m, total[48:])
        return carry

    lax.fori_loop(0, NC // 2, second, 0)

    def put(side, n):
        at = pl.multiple_of(side * COLS + n * CW, CW)
        return pltpu.make_async_copy(obuf.at[side, n], out_ref.at[:, pl.ds(at, CW)], osem.at[side, n])

    def last(m, carry):
        for side in (co, 1 - co):
            mine = side is co
            n = 2 * m + 1
            if not mine:
                send3(n).wait_recv()
            send2y(m, 0, side).wait_recv()
            total = own2[n, co] if mine else fm[n].astype(F32)
            obuf[side, n] = (total + f1[side, m].astype(F32)).astype(BF16)
            put(side, n).start()
            n = 2 * m
            if not mine:
                send3(n).wait_recv()
            total = own2[n, co] if mine else fm[n].astype(F32)
            for d in (1, 2, 3):
                send2x(m, d, 0, side).wait_recv()
                total = total + f0[side, d - 1, m].astype(F32)
            obuf[side, n] = total.astype(BF16)
            put(side, n).start()
        return carry

    lax.fori_loop(0, NC // 2, last, 0)

    def sent(m, carry):
        for d in (1, 2, 3):
            send1x(m, d).wait_send()
            for cc in (0, 1):
                send2x(m, d, cc, co).wait_send()
        send1y(m).wait_send()
        for cc in (0, 1):
            send2y(m, cc, co).wait_send()
        for kind in (0, 1):
            send3(2 * m + kind).wait_send()
        return carry

    lax.fori_loop(0, NC // 2, sent, 0)

    def stored(n, carry):
        for side in (0, 1):
            put(side, n).wait()
        return carry

    lax.fori_loop(0, NC, stored, 0)

    for copy in [q_copy, w_copy] + a_copies:
        copy.wait_send()
    for i in range(3):

        @pl.when(y_rows[i] > r)
        def _():
            y_copies[i].wait_send()

    def drain(d, carry):
        for j in range(4):
            for way in (0, 1):
                for step in (1,) if j else (2, 1):

                    @pl.when(goes(way, d, step, j))
                    def _():
                        hop(way, d, step, j).wait_send()

        return carry

    lax.fori_loop(0, 6, drain, 0)


def local(queries, key_rows, value_rows, block_flags, out_weight):
    dma = pltpu.SemaphoreType.DMA
    hbm = pl.BlockSpec(memory_space=pl.ANY)
    vmem = pltpu.VMEM
    return pl.pallas_call(
        kernel,
        out_shape=jax.ShapeDtypeStruct((8, 2 * COLS), BF16),
        in_specs=[hbm] * 5,
        out_specs=hbm,
        scratch_shapes=[
            pltpu.SMEM((2, 96), jnp.int32),
            vmem((2, NC, 8, CW), BF16),
            vmem((NZ, 4, HALF, 2 * HD), BF16),
            vmem((HALF, 2 * HD), BF16),
            vmem((2, TOK, 4 * HD), BF16),
            vmem((4, HD, 2 * TOK), BF16),
            vmem((2, HD, 4 * HALF), BF16),
            vmem((4, HD + 8, 2 * TOK), F32),
            vmem((4, HD + 8, 2 * TOK), F32),
            vmem((2, 8, 16, 8 * HD), BF16),
            vmem((2, 4 * HD, COLS), BF16),
            vmem((NC, 96, CW), BF16),
            vmem((NC, 64, CW), F32),
            vmem((NC // 2, 64, CW), BF16),
            vmem((3, NC // 2, 32, CW), BF16),
            vmem((NC // 2, 3, 2, 8, CW), BF16),
            vmem((NC // 2, 2, 8, CW), BF16),
            vmem((NC, 2, 8, CW), BF16),
            vmem((2, 3, NC // 2, 8, CW), BF16),
            vmem((2, NC // 2, 8, CW), BF16),
            vmem((NC, 8, CW), BF16),
            vmem((NC, 2, 8, CW), F32),
            dma((5,)),
            dma,
            dma,
            dma((2, NC)),
            dma((3,)),
            dma((3,)),
            dma((2, 6, 4)),
            dma((2, 6, 4)),
            dma((2,)),
            dma((2,)),
            dma((4,)),
            dma((4,)),
            dma((4, NC // 2)),
            dma((4, NC // 2)),
            dma((4, 2, NC // 2)),
            dma((2, 4, NC // 2)),
            dma((NC,)),
            dma((NC,)),
        ],
        compiler_params=pltpu.CompilerParams(
            collective_id=0, has_side_effects=True, vmem_limit_bytes=60 * 2**20
        ),
        name="attention_layer",
    )(queries, key_rows, value_rows, block_flags, out_weight)


def solution(mesh):
    placed = (P("ctx", "head"), P("ctx", None), P("ctx", None), P("ctx", None), P("head", None))
    return jax.shard_map(
        local, mesh=mesh, in_specs=placed, out_specs=P(("ctx", "head"), None), check_vma=False
    )
```

```python
import math

import jax
import jax.numpy as jnp
from jax import lax
from jax.experimental import pallas as pl
from jax.experimental.pallas import tpu as pltpu
from jax.sharding import PartitionSpec as P

MESH = pl.DeviceIdType.MESH
HD = 128
TOK = 128
HALF = 64
NZ = 12
NX = 4
NR = 4
COLS = 4096
CW = 512
NC = COLS // CW
SCALE = math.log2(math.e) / math.sqrt(HD)
NEG = 1e30
FLOOR = -1e20
F32 = jnp.float32
BF16 = jnp.bfloat16


def kernel(
    q_ref, k_ref, v_ref, flags_ref, w_ref, out_ref,
    flags, obuf, kv, oth, qall, qt, vt, acc, racc, a2, wv, sbuf, own, r1, r1x, s2a, s2b, s2d, f0, f1, fm, own2,
    lsem, wsem, fsem, osem, ytx, yrx, tx, rx, qsem, wrem, atx, arx, t1, q1, t2, q2, t3, q3,
):
    c = lax.axis_index("ctx")
    h = lax.axis_index("head")
    r, z = lax.div(c, NZ), lax.rem(c, NZ)
    x, yl, co = lax.div(h, 4), lax.rem(lax.div(h, 2), 2), lax.rem(h, 2)
    sg = 1 - 2 * yl

    def dev(rr, zz, xx, yy, cc):
        return {"ctx": rr * NZ + zz, "head": xx * 4 + yy * 2 + cc}

    zp = dev(r, lax.rem(z + 1, NZ), x, yl, co)
    zm = dev(r, lax.rem(z + NZ - 1, NZ), x, yl, co)
    r_minus, r_plus, r_far = lax.rem(r - sg + NR, NR), lax.rem(r + sg + NR, NR), lax.rem(r + 2, NR)
    dev_a = dev(r_minus, z, x, 1 - yl, co)
    dev_b = dev(r_minus, z, x, yl, co)
    dev_b_src = dev(r_plus, z, x, yl, co)
    dev_c = dev(r_far, z, x, 1 - yl, co)
    mate = dev(r, z, x, yl, 1 - co)

    def xdev(d, cc):
        return dev(r, z, lax.rem(x + d, NX), yl, cc)

    def ydev(cc):
        return dev(r, z, x, 1 - yl, cc)

    row_of = (r, r_minus, r_plus, r_far)

    head_own = x * 2 + yl
    head_oth = x * 2 + 1 - yl
    rows = pl.ds(pl.multiple_of(co * HALF, HALF), HALF)

    def head_cols(kvh):
        return pl.ds(pl.multiple_of(kvh * HD, HD), HD)

    loads = [
        pltpu.make_async_copy(k_ref.at[rows, head_cols(head_own)], kv.at[z, 0, :, pl.ds(0, HD)], lsem.at[0]),
        pltpu.make_async_copy(v_ref.at[rows, head_cols(head_own)], kv.at[z, 0, :, pl.ds(HD, HD)], lsem.at[1]),
        pltpu.make_async_copy(k_ref.at[rows, head_cols(head_oth)], oth.at[:, pl.ds(0, HD)], lsem.at[2]),
        pltpu.make_async_copy(v_ref.at[rows, head_cols(head_oth)], oth.at[:, pl.ds(HD, HD)], lsem.at[3]),
        pltpu.make_async_copy(q_ref, qall.at[co], lsem.at[4]),
    ]
    for copy in loads:
        copy.start()
    flag_load = pltpu.make_async_copy(flags_ref, flags, fsem)
    flag_load.start()
    w_own = pltpu.make_async_copy(
        w_ref.at[:, pl.ds(pl.multiple_of(co * COLS, COLS), COLS)], wv.at[co], wsem
    )
    w_own.start()

    barrier = pltpu.get_barrier_semaphore()
    peers = [zp, zm, dev_a, dev_b_src, dev_c, mate, ydev(0), ydev(1)]
    peers += [xdev(d, cc) for d in (1, 2, 3) for cc in (0, 1)]
    for peer in peers:
        pl.semaphore_signal(barrier, inc=1, device_id=peer, device_id_type=MESH)
    pl.semaphore_wait(barrier, len(peers))

    def remote(src, dst, send_sem, recv_sem, peer):
        return pltpu.make_async_remote_copy(
            src_ref=src, dst_ref=dst, send_sem=send_sem, recv_sem=recv_sem, device_id=peer, device_id_type=MESH
        )

    def at_plus(d):
        return lax.rem(z + NZ - d, NZ)

    def at_minus(d):
        return lax.rem(z + d, NZ)

    def hop(way, d, j):
        zi = at_plus(d) if way == 0 else at_minus(d)
        return remote(kv.at[zi, j], kv.at[zi, j], tx.at[way, d, j], rx.at[way, d, j], zp if way == 0 else zm)

    def arrival(way, d, j):
        zi = at_plus(d) if way == 0 else at_minus(d)
        return remote(kv.at[zi, j], kv.at[zi, j], tx.at[way, d - 1, j], rx.at[way, d - 1, j], zp if way == 0 else zm)

    def comes(zz, way, d, j):
        if j:
            return row_of[j] < r
        if way == 0:
            return zz >= d
        return (zz + d >= NZ) | (zz + d <= 4)

    def goes(way, d, j):
        return comes(lax.rem(z + 1, NZ) if way == 0 else lax.rem(z + NZ - 1, NZ), way, d + 1, j)

    def clear(zi, carry):
        @pl.when((zi > z) & (zi > 4))
        def _():
            kv[zi, 0] = jnp.zeros((HALF, 2 * HD), BF16)

        for j in (1, 2, 3):

            @pl.when(row_of[j] > r)
            def _():
                kv[zi, j] = jnp.zeros((HALF, 2 * HD), BF16)

        return carry

    for copy in loads[:2]:
        copy.wait()
    for way in (0, 1):

        @pl.when(goes(way, 0, 0))
        def _():
            hop(way, 0, 0).start()

    for copy in loads[2:4]:
        copy.wait()
    y_copies = [
        remote(oth, kv.at[z, 1], ytx.at[0], yrx.at[0], dev_a),
        remote(kv.at[z, 0], kv.at[z, 2], ytx.at[1], yrx.at[1], dev_b),
        remote(oth, kv.at[z, 3], ytx.at[2], yrx.at[2], dev_c),
    ]
    y_rows = (r_minus, r_minus, r_far)
    for i in (2, 1, 0):

        @pl.when(y_rows[i] > r)
        def _():
            y_copies[i].start()

    q_copy = remote(q_ref, qall.at[co], qsem.at[0], qsem.at[1], mate)
    q_copy.start()
    w_copy = remote(
        w_ref.at[:, pl.ds(pl.multiple_of((1 - co) * COLS, COLS), COLS)], wv.at[co], wrem.at[0], wrem.at[1], mate
    )
    w_copy.start()

    lane = lax.broadcasted_iota(jnp.int32, (1, 2 * TOK), 1)
    first_half = lax.rem(lane, TOK) < HALF

    loads[4].wait()
    q_copy.wait_recv()
    for i in range(8):
        side = slice((i % 2) * TOK, (i % 2 + 1) * TOK)
        qt[i // 2, :, side] = qall[i // 4, :, (i % 4) * HD : (i % 4 + 1) * HD].T
    for g in range(4):
        acc[g, :HD] = jnp.zeros((HD, 2 * TOK), F32)
        acc[g, HD : HD + 8] = jnp.where(
            lax.broadcasted_iota(jnp.int32, (8, 2 * TOK), 0) == 0, FLOOR, 0.0
        )

    def relay(way, d, j):
        last = 6 if (j < 2) == (way == 0) else 5

        @pl.when((d <= last) & comes(z, way, d, j))
        def _():
            arrival(way, d, j).wait_recv()

        @pl.when((d < last) & goes(way, d, j))
        def _():
            hop(way, d, j).start()

    for way in (0, 1):
        relay(way, 1, 0)
    for j in (1, 2, 3):

        @pl.when(row_of[j] < r)
        def _():
            y_copies[j - 1].wait_recv()
            hop(0, 0, j).start()
            hop(1, 0, j).start()

    lax.fori_loop(0, NZ, clear, 0)
    flag_load.wait()
    def prepare(slot, zi):
        vt[slot] = kv[zi, :, :, HD:].reshape(4 * HALF, HD).T

    def attend(bundles, g, diagonal=False):
        query = qt[g]
        old = acc[g, HD : HD + 1]
        new = old
        tiles = []
        for slot, zi in bundles:
            keys = kv[zi, :, :, :HD].reshape(4 * HALF, HD)
            scores = jnp.dot(keys, query, preferred_element_type=F32)
            parts = []
            for j in range(4):
                at = 2 * (row_of[j] * NZ + zi) + co
                flag = jnp.where(first_half, flags[0, at], flags[1, at]).astype(F32)
                bias = (flag - 1.0) * NEG
                if diagonal and j == 0:
                    key_pos = co * HALF + lax.broadcasted_iota(jnp.int32, (HALF, 2 * TOK), 0)
                    query_pos = lax.rem(lax.broadcasted_iota(jnp.int32, (HALF, 2 * TOK), 1), TOK)
                    bias = jnp.where(key_pos <= query_pos, bias, -NEG)
                parts.append(scores[j * HALF : (j + 1) * HALF] * SCALE + bias)
            scores = jnp.concatenate(parts, axis=0)
            new = jnp.maximum(new, jnp.max(scores, axis=0, keepdims=True))
            tiles.append(scores)
        factor = jnp.exp2(old - new)
        total = acc[g, HD + 1 : HD + 2] * factor
        mixed = acc[g, :HD] * factor
        for (slot, _), scores in zip(bundles, tiles):
            weights = jnp.exp2(scores - new)
            total = total + jnp.sum(weights, axis=0, keepdims=True)
            mixed = mixed + jnp.dot(vt[slot], weights.astype(BF16), preferred_element_type=F32)
        acc[g, HD : HD + 1] = new
        acc[g, HD + 1 : HD + 2] = total
        acc[g, :HD] = mixed

    def relays(k, j):
        for way in (0, 1):
            relay(way, k + 1 if j == 0 else k, j)

    for j in range(4):
        relays(1, j)
        if j == 0:
            prepare(0, z)
        attend([(0, z)], j, diagonal=True)

    def step(k, carry):
        for j in range(4):
            relays(k, j)
            if j == 0:
                prepare(0, at_plus(k - 1))
                prepare(1, at_minus(k - 1))
            attend([(0, at_plus(k - 1)), (1, at_minus(k - 1))], j)
        return carry

    lax.fori_loop(2, 7, step, 0)

    a_copies = [remote(acc.at[g], racc.at[g], atx.at[g], arx.at[g], mate) for g in range(4)]
    prepare(0, at_minus(6))
    for g in range(4):
        attend([(0, at_minus(6))], g)
        a_copies[g].start()

    def places(xx, yy):
        dx = lax.rem(xx - x + NX + 3, NX)
        near = lax.rem(yy + yl, 2)
        return dx + 4 * (1 - near), dx * 2 + near

    for g in range(4):
        a_copies[g].wait_recv()
        m0, m1 = acc[g, HD : HD + 1], racc[g, HD : HD + 1]
        top = jnp.maximum(m0, m1)
        e0, e1 = jnp.exp2(m0 - top), jnp.exp2(m1 - top)
        total = acc[g, HD + 1 : HD + 2] * e0 + racc[g, HD + 1 : HD + 2] * e1
        mixed = (acc[g, :HD] * e0 + racc[g, :HD] * e1) / total
        for i in (0, 1):
            tile = mixed[:, i * TOK : (i + 1) * TOK].T.astype(BF16)
            cols = slice((2 * g + i) * HD, (2 * g + i + 1) * HD)
            for xx in range(4):
                for yy in range(2):
                    at = (xx * 2 + yy) * 16
                    for kind, place in enumerate(places(xx, yy)):
                        a2[kind, place, :, cols] = tile[at : at + 16]

    w_own.wait()
    w_copy.wait_recv()

    def send1y(m):
        return remote(sbuf.at[2 * m, pl.ds(0, 64)], r1.at[m], t1.at[3, m], q1.at[3, m], ydev(co))

    def send1x(m, d):
        rows = pl.ds(32 * (d - 1), 32)
        return remote(sbuf.at[2 * m + 1, rows], r1x.at[d - 1, m], t1.at[d - 1, m], q1.at[d - 1, m], xdev(d, co))

    def project(m, carry):
        for kind in (1, 0):
            n = 2 * m + kind
            cols = pl.ds(pl.multiple_of(n * CW, CW), CW)
            part = jnp.dot(
                a2[kind].reshape(TOK, 8 * HD), wv[:, :, cols].reshape(8 * HD, CW), preferred_element_type=F32
            )
            sbuf[n] = part[:96].astype(BF16)
            own[n] = part[64:]
            if kind:
                for d in (2, 1, 3):
                    send1x(m, d).start()
            else:
                send1y(m).start()
        return carry

    lax.fori_loop(0, NC // 2, project, 0)

    def send2x(m, d, cc, side):
        return remote(s2a.at[m, d - 1, cc], f0.at[side, d - 1, m], t2.at[d - 1, cc, m], q2.at[side, d - 1, m], xdev(d, cc))

    def send2y(m, cc, side):
        return remote(s2b.at[m, cc], f1.at[side, m], t2.at[3, cc, m], q2.at[side, 3, m], ydev(cc))

    def send3(n):
        return remote(s2d.at[n, 1 - co], fm.at[n], t3.at[n], q3.at[n], mate)

    def keep(n, total):
        for cc in (0, 1):
            own2[n, cc] = total[8 * cc : 8 * cc + 8]
            s2d[n, cc] = total[8 * cc : 8 * cc + 8].astype(BF16)
        send3(n).start()

    def second(m, carry):
        for d in (1, 2, 3):
            send1x(m, d).wait_recv()
        total = own[2 * m + 1, pl.ds(32, 32)]
        for d in range(3):
            total = total + r1x[d, m].astype(F32)
        for cc in (0, 1):
            s2b[m, cc] = total[16 + 8 * cc : 24 + 8 * cc].astype(BF16)
            send2y(m, cc, co).start()
        keep(2 * m + 1, total[:16])
        send1y(m).wait_recv()
        total = own[2 * m] + r1[m].astype(F32)
        for d in (2, 1, 3):
            for cc in (0, 1):
                at = 16 * (d - 1) + 8 * cc
                s2a[m, d - 1, cc] = total[at : at + 8].astype(BF16)
                send2x(m, d, cc, co).start()
        keep(2 * m, total[48:])
        return carry

    lax.fori_loop(0, NC // 2, second, 0)

    def put(side, n):
        at = pl.multiple_of(side * COLS + n * CW, CW)
        return pltpu.make_async_copy(obuf.at[side, n], out_ref.at[:, pl.ds(at, CW)], osem.at[side, n])

    def last(m, carry):
        for side in (co, 1 - co):
            mine = side is co
            n = 2 * m + 1
            if not mine:
                send3(n).wait_recv()
            send2y(m, 0, side).wait_recv()
            total = own2[n, co] if mine else fm[n].astype(F32)
            obuf[side, n] = (total + f1[side, m].astype(F32)).astype(BF16)
            put(side, n).start()
            n = 2 * m
            if not mine:
                send3(n).wait_recv()
            total = own2[n, co] if mine else fm[n].astype(F32)
            for d in (1, 2, 3):
                send2x(m, d, 0, side).wait_recv()
                total = total + f0[side, d - 1, m].astype(F32)
            obuf[side, n] = total.astype(BF16)
            put(side, n).start()
        return carry

    lax.fori_loop(0, NC // 2, last, 0)

    def sent(m, carry):
        for d in (1, 2, 3):
            send1x(m, d).wait_send()
            for cc in (0, 1):
                send2x(m, d, cc, co).wait_send()
        send1y(m).wait_send()
        for cc in (0, 1):
            send2y(m, cc, co).wait_send()
        for kind in (0, 1):
            send3(2 * m + kind).wait_send()
        return carry

    lax.fori_loop(0, NC // 2, sent, 0)

    def stored(n, carry):
        for side in (0, 1):
            put(side, n).wait()
        return carry

    lax.fori_loop(0, NC, stored, 0)

    for copy in [q_copy, w_copy] + a_copies:
        copy.wait_send()
    for i in range(3):

        @pl.when(y_rows[i] > r)
        def _():
            y_copies[i].wait_send()

    def drain(d, carry):
        for j in range(4):
            for way in (0, 1):
                last = 6 if (j < 2) == (way == 0) else 5

                @pl.when((d < last) & goes(way, d, j))
                def _():
                    hop(way, d, j).wait_send()

        return carry

    lax.fori_loop(0, 6, drain, 0)


def local(queries, key_rows, value_rows, block_flags, out_weight):
    dma = pltpu.SemaphoreType.DMA
    hbm = pl.BlockSpec(memory_space=pl.ANY)
    vmem = pltpu.VMEM
    return pl.pallas_call(
        kernel,
        out_shape=jax.ShapeDtypeStruct((8, 2 * COLS), BF16),
        in_specs=[hbm] * 5,
        out_specs=hbm,
        scratch_shapes=[
            pltpu.SMEM((2, 96), jnp.int32),
            vmem((2, NC, 8, CW), BF16),
            vmem((NZ, 4, HALF, 2 * HD), BF16),
            vmem((HALF, 2 * HD), BF16),
            vmem((2, TOK, 4 * HD), BF16),
            vmem((4, HD, 2 * TOK), BF16),
            vmem((2, HD, 4 * HALF), BF16),
            vmem((4, HD + 8, 2 * TOK), F32),
            vmem((4, HD + 8, 2 * TOK), F32),
            vmem((2, 8, 16, 8 * HD), BF16),
            vmem((2, 4 * HD, COLS), BF16),
            vmem((NC, 96, CW), BF16),
            vmem((NC, 64, CW), F32),
            vmem((NC // 2, 64, CW), BF16),
            vmem((3, NC // 2, 32, CW), BF16),
            vmem((NC // 2, 3, 2, 8, CW), BF16),
            vmem((NC // 2, 2, 8, CW), BF16),
            vmem((NC, 2, 8, CW), BF16),
            vmem((2, 3, NC // 2, 8, CW), BF16),
            vmem((2, NC // 2, 8, CW), BF16),
            vmem((NC, 8, CW), BF16),
            vmem((NC, 2, 8, CW), F32),
            dma((5,)),
            dma,
            dma,
            dma((2, NC)),
            dma((3,)),
            dma((3,)),
            dma((2, 6, 4)),
            dma((2, 6, 4)),
            dma((2,)),
            dma((2,)),
            dma((4,)),
            dma((4,)),
            dma((4, NC // 2)),
            dma((4, NC // 2)),
            dma((4, 2, NC // 2)),
            dma((2, 4, NC // 2)),
            dma((NC,)),
            dma((NC,)),
        ],
        compiler_params=pltpu.CompilerParams(
            collective_id=0, has_side_effects=True, vmem_limit_bytes=60 * 2**20
        ),
        name="attention_layer",
    )(queries, key_rows, value_rows, block_flags, out_weight)


def solution(mesh):
    placed = (P("ctx", "head"), P("ctx", None), P("ctx", None), P("ctx", None), P("head", None))
    return jax.shard_map(
        local, mesh=mesh, in_specs=placed, out_specs=P(("ctx", "head"), None), check_vma=False
    )
```

```python
import math

import jax
import jax.numpy as jnp
from jax import lax
from jax.experimental import pallas as pl
from jax.experimental.pallas import tpu as pltpu
from jax.sharding import PartitionSpec as P

MESH = pl.DeviceIdType.MESH
HD = 128
TOK = 128
HALF = 64
NZ = 12
NX = 4
NR = 4
COLS = 4096
CW = 512
NC = COLS // CW
SCALE = math.log2(math.e) / math.sqrt(HD)
NEG = 1e30
FLOOR = -1e20
F32 = jnp.float32
BF16 = jnp.bfloat16


def kernel(
    q_ref, k_ref, v_ref, flags_ref, w_ref, out_ref,
    flags, obuf, kv, oth, qall, qt, vt, acc, racc, a2, wv, sbuf, own, r1, r1x, s2a, s2b, s2d, f0, f1, fm, own2,
    lsem, wsem, fsem, osem, ytx, yrx, tx, rx, qsem, wrem, atx, arx, t1, q1, t2, q2, t3, q3,
):
    c = lax.axis_index("ctx")
    h = lax.axis_index("head")
    r, z = lax.div(c, NZ), lax.rem(c, NZ)
    x, yl, co = lax.div(h, 4), lax.rem(lax.div(h, 2), 2), lax.rem(h, 2)
    sg = 1 - 2 * yl

    def dev(rr, zz, xx, yy, cc):
        return {"ctx": rr * NZ + zz, "head": xx * 4 + yy * 2 + cc}

    zp = dev(r, lax.rem(z + 1, NZ), x, yl, co)
    zm = dev(r, lax.rem(z + NZ - 1, NZ), x, yl, co)
    r_minus, r_plus, r_far = lax.rem(r - sg + NR, NR), lax.rem(r + sg + NR, NR), lax.rem(r + 2, NR)
    dev_a = dev(r_minus, z, x, 1 - yl, co)
    dev_b = dev(r_minus, z, x, yl, co)
    dev_b_src = dev(r_plus, z, x, yl, co)
    dev_c = dev(r_far, z, x, 1 - yl, co)
    mate = dev(r, z, x, yl, 1 - co)

    def xdev(d, cc):
        return dev(r, z, lax.rem(x + d, NX), yl, cc)

    def ydev(cc):
        return dev(r, z, x, 1 - yl, cc)

    row_of = (r, r_minus, r_plus, r_far)

    head_own = x * 2 + yl
    head_oth = x * 2 + 1 - yl
    rows = pl.ds(pl.multiple_of(co * HALF, HALF), HALF)

    def head_cols(kvh):
        return pl.ds(pl.multiple_of(kvh * HD, HD), HD)

    loads = [
        pltpu.make_async_copy(k_ref.at[rows, head_cols(head_own)], kv.at[z, 0, :, pl.ds(0, HD)], lsem.at[0]),
        pltpu.make_async_copy(v_ref.at[rows, head_cols(head_own)], kv.at[z, 0, :, pl.ds(HD, HD)], lsem.at[1]),
        pltpu.make_async_copy(k_ref.at[rows, head_cols(head_oth)], oth.at[:, pl.ds(0, HD)], lsem.at[2]),
        pltpu.make_async_copy(v_ref.at[rows, head_cols(head_oth)], oth.at[:, pl.ds(HD, HD)], lsem.at[3]),
        pltpu.make_async_copy(q_ref, qall.at[co], lsem.at[4]),
    ]
    for copy in loads:
        copy.start()
    flag_load = pltpu.make_async_copy(flags_ref, flags, fsem)
    flag_load.start()
    w_own = pltpu.make_async_copy(
        w_ref.at[:, pl.ds(pl.multiple_of(co * COLS, COLS), COLS)], wv.at[co], wsem
    )
    w_own.start()

    barrier = pltpu.get_barrier_semaphore()
    peers = [zp, zm, dev_a, dev_b_src, dev_c, mate, ydev(0), ydev(1)]
    peers += [xdev(d, cc) for d in (1, 2, 3) for cc in (0, 1)]
    for peer in peers:
        pl.semaphore_signal(barrier, inc=1, device_id=peer, device_id_type=MESH)
    pl.semaphore_wait(barrier, len(peers))

    def remote(src, dst, send_sem, recv_sem, peer):
        return pltpu.make_async_remote_copy(
            src_ref=src, dst_ref=dst, send_sem=send_sem, recv_sem=recv_sem, device_id=peer, device_id_type=MESH
        )

    def at_plus(d):
        return lax.rem(z + NZ - d, NZ)

    def at_minus(d):
        return lax.rem(z + d, NZ)

    def hop(way, d, j):
        zi = at_plus(d) if way == 0 else at_minus(d)
        return remote(kv.at[zi, j], kv.at[zi, j], tx.at[way, d, j], rx.at[way, d, j], zp if way == 0 else zm)

    def arrival(way, d, j):
        zi = at_plus(d) if way == 0 else at_minus(d)
        return remote(kv.at[zi, j], kv.at[zi, j], tx.at[way, d - 1, j], rx.at[way, d - 1, j], zp if way == 0 else zm)

    def comes(zz, way, d, j):
        if j:
            return row_of[j] < r
        if way == 0:
            return zz >= d
        return (zz + d >= NZ) | (zz + d <= 4)

    def farthest(way, j, zz):
        if j == 1:
            return jnp.where((zz > 5) == (way == 0), 6, 5)
        return 6 if (j < 2) == (way == 0) else 5

    def goes(way, d, j):
        zz = lax.rem(z + 1, NZ) if way == 0 else lax.rem(z + NZ - 1, NZ)
        return (d + 1 <= farthest(way, j, zz)) & comes(zz, way, d + 1, j)

    def clear(zi, carry):
        @pl.when((zi > z) & (zi > 4))
        def _():
            kv[zi, 0] = jnp.zeros((HALF, 2 * HD), BF16)

        for j in (1, 2, 3):

            @pl.when(row_of[j] > r)
            def _():
                kv[zi, j] = jnp.zeros((HALF, 2 * HD), BF16)

        return carry

    for copy in loads[:2]:
        copy.wait()
    for way in (0, 1):

        @pl.when(goes(way, 0, 0))
        def _():
            hop(way, 0, 0).start()

    for copy in loads[2:4]:
        copy.wait()
    y_copies = [
        remote(oth, kv.at[z, 1], ytx.at[0], yrx.at[0], dev_a),
        remote(kv.at[z, 0], kv.at[z, 2], ytx.at[1], yrx.at[1], dev_b),
        remote(oth, kv.at[z, 3], ytx.at[2], yrx.at[2], dev_c),
    ]
    y_rows = (r_minus, r_minus, r_far)
    for i in (0, 1, 2):

        @pl.when(y_rows[i] > r)
        def _():
            y_copies[i].start()

    q_copy = remote(q_ref, qall.at[co], qsem.at[0], qsem.at[1], mate)
    q_copy.start()
    w_copy = remote(
        w_ref.at[:, pl.ds(pl.multiple_of((1 - co) * COLS, COLS), COLS)], wv.at[co], wrem.at[0], wrem.at[1], mate
    )
    w_copy.start()

    lane = lax.broadcasted_iota(jnp.int32, (1, 2 * TOK), 1)
    first_half = lax.rem(lane, TOK) < HALF

    loads[4].wait()
    q_copy.wait_recv()
    for i in range(8):
        side = slice((i % 2) * TOK, (i % 2 + 1) * TOK)
        qt[i // 2, :, side] = qall[i // 4, :, (i % 4) * HD : (i % 4 + 1) * HD].T
    for g in range(4):
        acc[g, :HD] = jnp.zeros((HD, 2 * TOK), F32)
        acc[g, HD : HD + 8] = jnp.where(
            lax.broadcasted_iota(jnp.int32, (8, 2 * TOK), 0) == 0, FLOOR, 0.0
        )

    def relay(way, d, j):
        @pl.when((d <= farthest(way, j, z)) & comes(z, way, d, j))
        def _():
            arrival(way, d, j).wait_recv()

        @pl.when(goes(way, d, j))
        def _():
            hop(way, d, j).start()

    for way in (0, 1):
        relay(way, 1, 0)
    for j in (1, 2, 3):

        @pl.when(row_of[j] < r)
        def _():
            y_copies[j - 1].wait_recv()
            hop(0, 0, j).start()
            hop(1, 0, j).start()

    lax.fori_loop(0, NZ, clear, 0)
    flag_load.wait()
    def prepare(slot, zi):
        vt[slot] = kv[zi, :, :, HD:].reshape(4 * HALF, HD).T

    def attend(bundles, g, diagonal=False):
        query = qt[g]
        old = acc[g, HD : HD + 1]
        new = old
        tiles = []
        for slot, zi in bundles:
            keys = kv[zi, :, :, :HD].reshape(4 * HALF, HD)
            scores = jnp.dot(keys, query, preferred_element_type=F32)
            parts = []
            for j in range(4):
                at = 2 * (row_of[j] * NZ + zi) + co
                flag = jnp.where(first_half, flags[0, at], flags[1, at]).astype(F32)
                bias = (flag - 1.0) * NEG
                if diagonal and j == 0:
                    key_pos = co * HALF + lax.broadcasted_iota(jnp.int32, (HALF, 2 * TOK), 0)
                    query_pos = lax.rem(lax.broadcasted_iota(jnp.int32, (HALF, 2 * TOK), 1), TOK)
                    bias = jnp.where(key_pos <= query_pos, bias, -NEG)
                parts.append(scores[j * HALF : (j + 1) * HALF] * SCALE + bias)
            scores = jnp.concatenate(parts, axis=0)
            new = jnp.maximum(new, jnp.max(scores, axis=0, keepdims=True))
            tiles.append(scores)
        factor = jnp.exp2(old - new)
        total = acc[g, HD + 1 : HD + 2] * factor
        mixed = acc[g, :HD] * factor
        for (slot, _), scores in zip(bundles, tiles):
            weights = jnp.exp2(scores - new)
            total = total + jnp.sum(weights, axis=0, keepdims=True)
            mixed = mixed + jnp.dot(vt[slot], weights.astype(BF16), preferred_element_type=F32)
        acc[g, HD : HD + 1] = new
        acc[g, HD + 1 : HD + 2] = total
        acc[g, :HD] = mixed

    def relays(k, j):
        for way in (0, 1):
            relay(way, k + 1 if j == 0 else k, j)

    for j in range(4):
        relays(1, j)
        if j == 0:
            prepare(0, z)
        attend([(0, z)], j, diagonal=True)

    def step(k, carry):
        for j in range(4):
            relays(k, j)
            if j == 0:
                prepare(0, at_plus(k - 1))
                prepare(1, at_minus(k - 1))
            attend([(0, at_plus(k - 1)), (1, at_minus(k - 1))], j)
        return carry

    lax.fori_loop(2, 7, step, 0)

    a_copies = [remote(acc.at[g], racc.at[g], atx.at[g], arx.at[g], mate) for g in range(4)]
    prepare(0, at_minus(6))
    for g in range(4):
        attend([(0, at_minus(6))], g)
        a_copies[g].start()

    def places(xx, yy):
        dx = lax.rem(xx - x + NX + 3, NX)
        near = lax.rem(yy + yl, 2)
        return dx + 4 * (1 - near), dx * 2 + near

    for g in range(4):
        a_copies[g].wait_recv()
        m0, m1 = acc[g, HD : HD + 1], racc[g, HD : HD + 1]
        top = jnp.maximum(m0, m1)
        e0, e1 = jnp.exp2(m0 - top), jnp.exp2(m1 - top)
        total = acc[g, HD + 1 : HD + 2] * e0 + racc[g, HD + 1 : HD + 2] * e1
        mixed = (acc[g, :HD] * e0 + racc[g, :HD] * e1) / total
        for i in (0, 1):
            tile = mixed[:, i * TOK : (i + 1) * TOK].T.astype(BF16)
            cols = slice((2 * g + i) * HD, (2 * g + i + 1) * HD)
            for xx in range(4):
                for yy in range(2):
                    at = (xx * 2 + yy) * 16
                    for kind, place in enumerate(places(xx, yy)):
                        a2[kind, place, :, cols] = tile[at : at + 16]

    w_own.wait()
    w_copy.wait_recv()

    def send1y(m):
        return remote(sbuf.at[2 * m, pl.ds(0, 64)], r1.at[m], t1.at[3, m], q1.at[3, m], ydev(co))

    def send1x(m, d):
        rows = pl.ds(32 * (d - 1), 32)
        return remote(sbuf.at[2 * m + 1, rows], r1x.at[d - 1, m], t1.at[d - 1, m], q1.at[d - 1, m], xdev(d, co))

    def project(m, carry):
        for kind in (1, 0):
            n = 2 * m + kind
            cols = pl.ds(pl.multiple_of(n * CW, CW), CW)
            part = jnp.dot(
                a2[kind].reshape(TOK, 8 * HD), wv[:, :, cols].reshape(8 * HD, CW), preferred_element_type=F32
            )
            sbuf[n] = part[:96].astype(BF16)
            own[n] = part[64:]
            if kind:
                for d in (2, 1, 3):
                    send1x(m, d).start()
            else:
                send1y(m).start()
        return carry

    lax.fori_loop(0, NC // 2, project, 0)

    def send2x(m, d, cc, side):
        return remote(s2a.at[m, d - 1, cc], f0.at[side, d - 1, m], t2.at[d - 1, cc, m], q2.at[side, d - 1, m], xdev(d, cc))

    def send2y(m, cc, side):
        return remote(s2b.at[m, cc], f1.at[side, m], t2.at[3, cc, m], q2.at[side, 3, m], ydev(cc))

    def send3(n):
        return remote(s2d.at[n, 1 - co], fm.at[n], t3.at[n], q3.at[n], mate)

    def keep(n, total):
        for cc in (0, 1):
            own2[n, cc] = total[8 * cc : 8 * cc + 8]
            s2d[n, cc] = total[8 * cc : 8 * cc + 8].astype(BF16)
        send3(n).start()

    def second(m, carry):
        for d in (1, 2, 3):
            send1x(m, d).wait_recv()
        total = own[2 * m + 1, pl.ds(32, 32)]
        for d in range(3):
            total = total + r1x[d, m].astype(F32)
        for cc in (0, 1):
            s2b[m, cc] = total[16 + 8 * cc : 24 + 8 * cc].astype(BF16)
            send2y(m, cc, co).start()
        keep(2 * m + 1, total[:16])
        send1y(m).wait_recv()
        total = own[2 * m] + r1[m].astype(F32)
        for d in (2, 1, 3):
            for cc in (0, 1):
                at = 16 * (d - 1) + 8 * cc
                s2a[m, d - 1, cc] = total[at : at + 8].astype(BF16)
                send2x(m, d, cc, co).start()
        keep(2 * m, total[48:])
        return carry

    lax.fori_loop(0, NC // 2, second, 0)

    def put(side, n):
        at = pl.multiple_of(side * COLS + n * CW, CW)
        return pltpu.make_async_copy(obuf.at[side, n], out_ref.at[:, pl.ds(at, CW)], osem.at[side, n])

    def last(m, carry):
        for side in (co, 1 - co):
            mine = side is co
            n = 2 * m + 1
            if not mine:
                send3(n).wait_recv()
            send2y(m, 0, side).wait_recv()
            total = own2[n, co] if mine else fm[n].astype(F32)
            obuf[side, n] = (total + f1[side, m].astype(F32)).astype(BF16)
            put(side, n).start()
            n = 2 * m
            if not mine:
                send3(n).wait_recv()
            total = own2[n, co] if mine else fm[n].astype(F32)
            for d in (1, 2, 3):
                send2x(m, d, 0, side).wait_recv()
                total = total + f0[side, d - 1, m].astype(F32)
            obuf[side, n] = total.astype(BF16)
            put(side, n).start()
        return carry

    lax.fori_loop(0, NC // 2, last, 0)

    def sent(m, carry):
        for d in (1, 2, 3):
            send1x(m, d).wait_send()
            for cc in (0, 1):
                send2x(m, d, cc, co).wait_send()
        send1y(m).wait_send()
        for cc in (0, 1):
            send2y(m, cc, co).wait_send()
        for kind in (0, 1):
            send3(2 * m + kind).wait_send()
        return carry

    lax.fori_loop(0, NC // 2, sent, 0)

    def stored(n, carry):
        for side in (0, 1):
            put(side, n).wait()
        return carry

    lax.fori_loop(0, NC, stored, 0)

    for copy in [q_copy, w_copy] + a_copies:
        copy.wait_send()
    for i in range(3):

        @pl.when(y_rows[i] > r)
        def _():
            y_copies[i].wait_send()

    def drain(d, carry):
        for j in range(4):
            for way in (0, 1):
                @pl.when(goes(way, d, j))
                def _():
                    hop(way, d, j).wait_send()

        return carry

    lax.fori_loop(0, 6, drain, 0)


def local(queries, key_rows, value_rows, block_flags, out_weight):
    dma = pltpu.SemaphoreType.DMA
    hbm = pl.BlockSpec(memory_space=pl.ANY)
    vmem = pltpu.VMEM
    return pl.pallas_call(
        kernel,
        out_shape=jax.ShapeDtypeStruct((8, 2 * COLS), BF16),
        in_specs=[hbm] * 5,
        out_specs=hbm,
        scratch_shapes=[
            pltpu.SMEM((2, 96), jnp.int32),
            vmem((2, NC, 8, CW), BF16),
            vmem((NZ, 4, HALF, 2 * HD), BF16),
            vmem((HALF, 2 * HD), BF16),
            vmem((2, TOK, 4 * HD), BF16),
            vmem((4, HD, 2 * TOK), BF16),
            vmem((2, HD, 4 * HALF), BF16),
            vmem((4, HD + 8, 2 * TOK), F32),
            vmem((4, HD + 8, 2 * TOK), F32),
            vmem((2, 8, 16, 8 * HD), BF16),
            vmem((2, 4 * HD, COLS), BF16),
            vmem((NC, 96, CW), BF16),
            vmem((NC, 64, CW), F32),
            vmem((NC // 2, 64, CW), BF16),
            vmem((3, NC // 2, 32, CW), BF16),
            vmem((NC // 2, 3, 2, 8, CW), BF16),
            vmem((NC // 2, 2, 8, CW), BF16),
            vmem((NC, 2, 8, CW), BF16),
            vmem((2, 3, NC // 2, 8, CW), BF16),
            vmem((2, NC // 2, 8, CW), BF16),
            vmem((NC, 8, CW), BF16),
            vmem((NC, 2, 8, CW), F32),
            dma((5,)),
            dma,
            dma,
            dma((2, NC)),
            dma((3,)),
            dma((3,)),
            dma((2, 6, 4)),
            dma((2, 6, 4)),
            dma((2,)),
            dma((2,)),
            dma((4,)),
            dma((4,)),
            dma((4, NC // 2)),
            dma((4, NC // 2)),
            dma((4, 2, NC // 2)),
            dma((2, 4, NC // 2)),
            dma((NC,)),
            dma((NC,)),
        ],
        compiler_params=pltpu.CompilerParams(
            collective_id=0, has_side_effects=True, vmem_limit_bytes=60 * 2**20
        ),
        name="attention_layer",
    )(queries, key_rows, value_rows, block_flags, out_weight)


def solution(mesh):
    placed = (P("ctx", "head"), P("ctx", None), P("ctx", None), P("ctx", None), P("head", None))
    return jax.shard_map(
        local, mesh=mesh, in_specs=placed, out_specs=P(("ctx", "head"), None), check_vma=False
    )
```

```python
import math

import jax
import jax.numpy as jnp
from jax import lax
from jax.experimental import pallas as pl
from jax.experimental.pallas import tpu as pltpu
from jax.sharding import PartitionSpec as P

MESH = pl.DeviceIdType.MESH
HD = 128
TOK = 128
HALF = 64
NZ = 12
NX = 4
NR = 4
COLS = 4096
CW = 512
NC = COLS // CW
SCALE = math.log2(math.e) / math.sqrt(HD)
NEG = 1e30
FLOOR = -1e20
F32 = jnp.float32
BF16 = jnp.bfloat16


def kernel(
    q_ref, k_ref, v_ref, flags_ref, w_ref, out_ref,
    flags, obuf, kv, oth, qall, qt, vt, acc, racc, a2, wv, sbuf, own, r1, r1x, s2a, s2b, s2d, f0, f1, fm, own2,
    lsem, wsem, fsem, osem, ytx, yrx, tx, rx, qsem, wrem, atx, arx, t1, q1, t2, q2, t3, q3,
):
    c = lax.axis_index("ctx")
    h = lax.axis_index("head")
    r, z = lax.div(c, NZ), lax.rem(c, NZ)
    x, yl, co = lax.div(h, 4), lax.rem(lax.div(h, 2), 2), lax.rem(h, 2)
    sg = 1 - 2 * yl

    def dev(rr, zz, xx, yy, cc):
        return {"ctx": rr * NZ + zz, "head": xx * 4 + yy * 2 + cc}

    zp = dev(r, lax.rem(z + 1, NZ), x, yl, co)
    zm = dev(r, lax.rem(z + NZ - 1, NZ), x, yl, co)
    r_minus, r_plus, r_far = lax.rem(r - sg + NR, NR), lax.rem(r + sg + NR, NR), lax.rem(r + 2, NR)
    dev_a = dev(r_minus, z, x, 1 - yl, co)
    dev_b = dev(r_minus, z, x, yl, co)
    dev_b_src = dev(r_plus, z, x, yl, co)
    dev_c = dev(r_far, z, x, 1 - yl, co)
    mate = dev(r, z, x, yl, 1 - co)

    def xdev(d, cc):
        return dev(r, z, lax.rem(x + d, NX), yl, cc)

    def ydev(cc):
        return dev(r, z, x, 1 - yl, cc)

    row_of = (r, r_minus, r_plus, r_far)

    head_own = x * 2 + yl
    head_oth = x * 2 + 1 - yl
    rows = pl.ds(pl.multiple_of(co * HALF, HALF), HALF)

    def head_cols(kvh):
        return pl.ds(pl.multiple_of(kvh * HD, HD), HD)

    loads = [
        pltpu.make_async_copy(k_ref.at[rows, head_cols(head_own)], kv.at[z, 0, :, pl.ds(0, HD)], lsem.at[0]),
        pltpu.make_async_copy(v_ref.at[rows, head_cols(head_own)], kv.at[z, 0, :, pl.ds(HD, HD)], lsem.at[1]),
        pltpu.make_async_copy(k_ref.at[rows, head_cols(head_oth)], oth.at[:, pl.ds(0, HD)], lsem.at[2]),
        pltpu.make_async_copy(v_ref.at[rows, head_cols(head_oth)], oth.at[:, pl.ds(HD, HD)], lsem.at[3]),
        pltpu.make_async_copy(q_ref, qall.at[co], lsem.at[4]),
    ]
    for copy in loads:
        copy.start()
    flag_load = pltpu.make_async_copy(flags_ref, flags, fsem)
    flag_load.start()
    w_own = pltpu.make_async_copy(
        w_ref.at[:, pl.ds(pl.multiple_of(co * COLS, COLS), COLS)], wv.at[co], wsem
    )
    w_own.start()

    barrier = pltpu.get_barrier_semaphore()
    peers = [zp, zm, dev_a, dev_b_src, dev_c, mate, ydev(0), ydev(1)]
    peers += [xdev(d, cc) for d in (1, 2, 3) for cc in (0, 1)]
    for peer in peers:
        pl.semaphore_signal(barrier, inc=1, device_id=peer, device_id_type=MESH)
    def clear(zi, carry):
        @pl.when((zi > z) & (zi > 4))
        def _():
            kv[zi, 0] = jnp.zeros((HALF, 2 * HD), BF16)

        for j in (1, 2, 3):

            @pl.when(row_of[j] > r)
            def _():
                kv[zi, j] = jnp.zeros((HALF, 2 * HD), BF16)

        return carry

    lax.fori_loop(0, NZ, clear, 0)
    for g in range(4):
        acc[g, :HD] = jnp.zeros((HD, 2 * TOK), F32)
        acc[g, HD : HD + 8] = jnp.where(
            lax.broadcasted_iota(jnp.int32, (8, 2 * TOK), 0) == 0, FLOOR, 0.0
        )
    pl.semaphore_wait(barrier, len(peers))

    def remote(src, dst, send_sem, recv_sem, peer):
        return pltpu.make_async_remote_copy(
            src_ref=src, dst_ref=dst, send_sem=send_sem, recv_sem=recv_sem, device_id=peer, device_id_type=MESH
        )

    def at_plus(d):
        return lax.rem(z + NZ - d, NZ)

    def at_minus(d):
        return lax.rem(z + d, NZ)

    def hop(way, d, j):
        zi = at_plus(d) if way == 0 else at_minus(d)
        return remote(kv.at[zi, j], kv.at[zi, j], tx.at[way, d, j], rx.at[way, d, j], zp if way == 0 else zm)

    def arrival(way, d, j):
        zi = at_plus(d) if way == 0 else at_minus(d)
        return remote(kv.at[zi, j], kv.at[zi, j], tx.at[way, d - 1, j], rx.at[way, d - 1, j], zp if way == 0 else zm)

    def comes(zz, way, d, j):
        if j:
            return row_of[j] < r
        if way == 0:
            return zz >= d
        return (zz + d >= NZ) | (zz + d <= 4)

    def farthest(way, j, zz):
        if j == 1:
            return jnp.where((zz > 5) == (way == 0), 6, 5)
        return 6 if (j < 2) == (way == 0) else 5

    def goes(way, d, j):
        zz = lax.rem(z + 1, NZ) if way == 0 else lax.rem(z + NZ - 1, NZ)
        return (d + 1 <= farthest(way, j, zz)) & comes(zz, way, d + 1, j)

    for copy in loads[:2]:
        copy.wait()
    for way in (0, 1):

        @pl.when(goes(way, 0, 0))
        def _():
            hop(way, 0, 0).start()

    for copy in loads[2:4]:
        copy.wait()
    y_copies = [
        remote(oth, kv.at[z, 1], ytx.at[0], yrx.at[0], dev_a),
        remote(kv.at[z, 0], kv.at[z, 2], ytx.at[1], yrx.at[1], dev_b),
        remote(oth, kv.at[z, 3], ytx.at[2], yrx.at[2], dev_c),
    ]
    y_rows = (r_minus, r_minus, r_far)
    for i in (0, 1, 2):

        @pl.when(y_rows[i] > r)
        def _():
            y_copies[i].start()

    q_copy = remote(q_ref, qall.at[co], qsem.at[0], qsem.at[1], mate)
    q_copy.start()
    w_copy = remote(
        w_ref.at[:, pl.ds(pl.multiple_of((1 - co) * COLS, COLS), COLS)], wv.at[co], wrem.at[0], wrem.at[1], mate
    )
    w_copy.start()

    lane = lax.broadcasted_iota(jnp.int32, (1, 2 * TOK), 1)
    first_half = lax.rem(lane, TOK) < HALF

    loads[4].wait()
    q_copy.wait_recv()
    for i in range(8):
        side = slice((i % 2) * TOK, (i % 2 + 1) * TOK)
        qt[i // 2, :, side] = qall[i // 4, :, (i % 4) * HD : (i % 4 + 1) * HD].T

    def relay(way, d, j):
        @pl.when((d <= farthest(way, j, z)) & comes(z, way, d, j))
        def _():
            arrival(way, d, j).wait_recv()

        @pl.when(goes(way, d, j))
        def _():
            hop(way, d, j).start()

    for way in (0, 1):
        relay(way, 1, 0)
    for j in (1, 2, 3):

        @pl.when(row_of[j] < r)
        def _():
            y_copies[j - 1].wait_recv()
            hop(0, 0, j).start()
            hop(1, 0, j).start()

    flag_load.wait()
    def prepare(slot, zi):
        vt[slot] = kv[zi, :, :, HD:].reshape(4 * HALF, HD).T

    def attend(bundles, g, diagonal=False):
        query = qt[g]
        old = acc[g, HD : HD + 1]
        new = old
        tiles = []
        for slot, zi in bundles:
            keys = kv[zi, :, :, :HD].reshape(4 * HALF, HD)
            scores = jnp.dot(keys, query, preferred_element_type=F32)
            parts = []
            for j in range(4):
                at = 2 * (row_of[j] * NZ + zi) + co
                flag = jnp.where(first_half, flags[0, at], flags[1, at]).astype(F32)
                bias = (flag - 1.0) * NEG
                if diagonal and j == 0:
                    key_pos = co * HALF + lax.broadcasted_iota(jnp.int32, (HALF, 2 * TOK), 0)
                    query_pos = lax.rem(lax.broadcasted_iota(jnp.int32, (HALF, 2 * TOK), 1), TOK)
                    bias = jnp.where(key_pos <= query_pos, bias, -NEG)
                parts.append(scores[j * HALF : (j + 1) * HALF] * SCALE + bias)
            scores = jnp.concatenate(parts, axis=0)
            new = jnp.maximum(new, jnp.max(scores, axis=0, keepdims=True))
            tiles.append(scores)
        factor = jnp.exp2(old - new)
        total = acc[g, HD + 1 : HD + 2] * factor
        mixed = acc[g, :HD] * factor
        for (slot, _), scores in zip(bundles, tiles):
            weights = jnp.exp2(scores - new)
            total = total + jnp.sum(weights, axis=0, keepdims=True)
            mixed = mixed + jnp.dot(vt[slot], weights.astype(BF16), preferred_element_type=F32)
        acc[g, HD : HD + 1] = new
        acc[g, HD + 1 : HD + 2] = total
        acc[g, :HD] = mixed

    def relays(k, j):
        for way in (0, 1):
            relay(way, k + 1 if j == 0 else k, j)

    for j in range(4):
        relays(1, j)
        if j == 0:
            prepare(0, z)
        attend([(0, z)], j, diagonal=True)

    def step(k, carry):
        for j in range(4):
            relays(k, j)
            if j == 0:
                prepare(0, at_plus(k - 1))
                prepare(1, at_minus(k - 1))
            attend([(0, at_plus(k - 1)), (1, at_minus(k - 1))], j)
        return carry

    lax.fori_loop(2, 7, step, 0)

    a_copies = [remote(acc.at[g], racc.at[g], atx.at[g], arx.at[g], mate) for g in range(4)]
    prepare(0, at_minus(6))
    for g in range(4):
        attend([(0, at_minus(6))], g)
        a_copies[g].start()

    def places(xx, yy):
        dx = lax.rem(xx - x + NX + 3, NX)
        near = lax.rem(yy + yl, 2)
        return dx + 4 * (1 - near), dx * 2 + near

    for g in range(4):
        a_copies[g].wait_recv()
        m0, m1 = acc[g, HD : HD + 1], racc[g, HD : HD + 1]
        top = jnp.maximum(m0, m1)
        e0, e1 = jnp.exp2(m0 - top), jnp.exp2(m1 - top)
        total = acc[g, HD + 1 : HD + 2] * e0 + racc[g, HD + 1 : HD + 2] * e1
        mixed = (acc[g, :HD] * e0 + racc[g, :HD] * e1) / total
        for i in (0, 1):
            tile = mixed[:, i * TOK : (i + 1) * TOK].T.astype(BF16)
            cols = slice((2 * g + i) * HD, (2 * g + i + 1) * HD)
            for xx in range(4):
                for yy in range(2):
                    at = (xx * 2 + yy) * 16
                    for kind, place in enumerate(places(xx, yy)):
                        a2[kind, place, :, cols] = tile[at : at + 16]

    w_own.wait()
    w_copy.wait_recv()

    def send1y(m):
        return remote(sbuf.at[2 * m, pl.ds(0, 64)], r1.at[m], t1.at[3, m], q1.at[3, m], ydev(co))

    def send1x(m, d):
        rows = pl.ds(32 * (d - 1), 32)
        return remote(sbuf.at[2 * m + 1, rows], r1x.at[d - 1, m], t1.at[d - 1, m], q1.at[d - 1, m], xdev(d, co))

    def project(m, carry):
        for kind in (1, 0):
            n = 2 * m + kind
            cols = pl.ds(pl.multiple_of(n * CW, CW), CW)
            part = jnp.dot(
                a2[kind].reshape(TOK, 8 * HD), wv[:, :, cols].reshape(8 * HD, CW), preferred_element_type=F32
            )
            sbuf[n] = part[:96].astype(BF16)
            own[n] = part[64:]
            if kind:
                for d in (2, 1, 3):
                    send1x(m, d).start()
            else:
                send1y(m).start()
        return carry

    lax.fori_loop(0, NC // 2, project, 0)

    def send2x(m, d, cc, side):
        return remote(s2a.at[m, d - 1, cc], f0.at[side, d - 1, m], t2.at[d - 1, cc, m], q2.at[side, d - 1, m], xdev(d, cc))

    def send2y(m, cc, side):
        return remote(s2b.at[m, cc], f1.at[side, m], t2.at[3, cc, m], q2.at[side, 3, m], ydev(cc))

    def send3(n):
        return remote(s2d.at[n, 1 - co], fm.at[n], t3.at[n], q3.at[n], mate)

    def keep(n, total):
        for cc in (0, 1):
            own2[n, cc] = total[8 * cc : 8 * cc + 8]
            s2d[n, cc] = total[8 * cc : 8 * cc + 8].astype(BF16)
        send3(n).start()

    def second(m, carry):
        for d in (1, 2, 3):
            send1x(m, d).wait_recv()
        total = own[2 * m + 1, pl.ds(32, 32)]
        for d in range(3):
            total = total + r1x[d, m].astype(F32)
        for cc in (0, 1):
            s2b[m, cc] = total[16 + 8 * cc : 24 + 8 * cc].astype(BF16)
            send2y(m, cc, co).start()
        keep(2 * m + 1, total[:16])
        send1y(m).wait_recv()
        total = own[2 * m] + r1[m].astype(F32)
        for d in (2, 1, 3):
            for cc in (0, 1):
                at = 16 * (d - 1) + 8 * cc
                s2a[m, d - 1, cc] = total[at : at + 8].astype(BF16)
                send2x(m, d, cc, co).start()
        keep(2 * m, total[48:])
        return carry

    lax.fori_loop(0, NC // 2, second, 0)

    def put(side, n):
        at = pl.multiple_of(side * COLS + n * CW, CW)
        return pltpu.make_async_copy(obuf.at[side, n], out_ref.at[:, pl.ds(at, CW)], osem.at[side, n])

    def last(m, carry):
        for side in (co, 1 - co):
            mine = side is co
            n = 2 * m + 1
            if not mine:
                send3(n).wait_recv()
            send2y(m, 0, side).wait_recv()
            total = own2[n, co] if mine else fm[n].astype(F32)
            obuf[side, n] = (total + f1[side, m].astype(F32)).astype(BF16)
            put(side, n).start()
            n = 2 * m
            if not mine:
                send3(n).wait_recv()
            total = own2[n, co] if mine else fm[n].astype(F32)
            for d in (1, 2, 3):
                send2x(m, d, 0, side).wait_recv()
                total = total + f0[side, d - 1, m].astype(F32)
            obuf[side, n] = total.astype(BF16)
            put(side, n).start()
        return carry

    lax.fori_loop(0, NC // 2, last, 0)

    def sent(m, carry):
        for d in (1, 2, 3):
            send1x(m, d).wait_send()
            for cc in (0, 1):
                send2x(m, d, cc, co).wait_send()
        send1y(m).wait_send()
        for cc in (0, 1):
            send2y(m, cc, co).wait_send()
        for kind in (0, 1):
            send3(2 * m + kind).wait_send()
        return carry

    lax.fori_loop(0, NC // 2, sent, 0)

    def stored(n, carry):
        for side in (0, 1):
            put(side, n).wait()
        return carry

    lax.fori_loop(0, NC, stored, 0)

    for copy in [q_copy, w_copy] + a_copies:
        copy.wait_send()
    for i in range(3):

        @pl.when(y_rows[i] > r)
        def _():
            y_copies[i].wait_send()

    def drain(d, carry):
        for j in range(4):
            for way in (0, 1):
                @pl.when(goes(way, d, j))
                def _():
                    hop(way, d, j).wait_send()

        return carry

    lax.fori_loop(0, 6, drain, 0)


def local(queries, key_rows, value_rows, block_flags, out_weight):
    dma = pltpu.SemaphoreType.DMA
    hbm = pl.BlockSpec(memory_space=pl.ANY)
    vmem = pltpu.VMEM
    return pl.pallas_call(
        kernel,
        out_shape=jax.ShapeDtypeStruct((8, 2 * COLS), BF16),
        in_specs=[hbm] * 5,
        out_specs=hbm,
        scratch_shapes=[
            pltpu.SMEM((2, 96), jnp.int32),
            vmem((2, NC, 8, CW), BF16),
            vmem((NZ, 4, HALF, 2 * HD), BF16),
            vmem((HALF, 2 * HD), BF16),
            vmem((2, TOK, 4 * HD), BF16),
            vmem((4, HD, 2 * TOK), BF16),
            vmem((2, HD, 4 * HALF), BF16),
            vmem((4, HD + 8, 2 * TOK), F32),
            vmem((4, HD + 8, 2 * TOK), F32),
            vmem((2, 8, 16, 8 * HD), BF16),
            vmem((2, 4 * HD, COLS), BF16),
            vmem((NC, 96, CW), BF16),
            vmem((NC, 64, CW), F32),
            vmem((NC // 2, 64, CW), BF16),
            vmem((3, NC // 2, 32, CW), BF16),
            vmem((NC // 2, 3, 2, 8, CW), BF16),
            vmem((NC // 2, 2, 8, CW), BF16),
            vmem((NC, 2, 8, CW), BF16),
            vmem((2, 3, NC // 2, 8, CW), BF16),
            vmem((2, NC // 2, 8, CW), BF16),
            vmem((NC, 8, CW), BF16),
            vmem((NC, 2, 8, CW), F32),
            dma((5,)),
            dma,
            dma,
            dma((2, NC)),
            dma((3,)),
            dma((3,)),
            dma((2, 6, 4)),
            dma((2, 6, 4)),
            dma((2,)),
            dma((2,)),
            dma((4,)),
            dma((4,)),
            dma((4, NC // 2)),
            dma((4, NC // 2)),
            dma((4, 2, NC // 2)),
            dma((2, 4, NC // 2)),
            dma((NC,)),
            dma((NC,)),
        ],
        compiler_params=pltpu.CompilerParams(
            collective_id=0, has_side_effects=True, vmem_limit_bytes=60 * 2**20
        ),
        name="attention_layer",
    )(queries, key_rows, value_rows, block_flags, out_weight)


def solution(mesh):
    placed = (P("ctx", "head"), P("ctx", None), P("ctx", None), P("ctx", None), P("head", None))
    return jax.shard_map(
        local, mesh=mesh, in_specs=placed, out_specs=P(("ctx", "head"), None), check_vma=False
    )
```
